32 devices in a mesh: slides: 2 (over y), row: 4 (over z), col: 4 (over x, core).
Axes of the slice: x: 2, y: 2, z: 4, core: 2. Of those that a mesh axis runs over, the one named last changes fastest.
Arguments:
- query_rows: bfloat16 [4096, 768], P(('slides', 'row', 'col')), parts along dimension 0, may hold values from -10 to 10
- key_rows: bfloat16 [4096, 768], P(('slides', 'row', 'col')), parts along dimension 0, may hold values from -10 to 10
- value_rows: bfloat16 [4096, 768], P(('slides', 'row', 'col')), parts along dimension 0, may hold values from -6 to 6
- out_grad: bfloat16 [4096, 768], P(('slides', 'row', 'col')), parts along dimension 0, may hold values from -6 to 6
- tissue: int32 [64], P('slides'), parts along dimension 0, may hold values from 0 to 1, as said below
- w_out: bfloat16 [768, 768], replicated, may hold values from -0.21875 to 0.21875
Outputs:
- output: bfloat16 [4096, 768], P(('slides', 'row', 'col')), parts along dimension 0
- query_grad: bfloat16 [4096, 768], P(('slides', 'row', 'col')), parts along dimension 0
- key_grad: bfloat16 [4096, 768], P(('slides', 'row', 'col')), parts along dimension 0
- value_grad: bfloat16 [4096, 768], P(('slides', 'row', 'col')), parts along dimension 0
- weight_grad: float32 [1536, 768], P('slides', 'row'), parts along dimension 0
The draws below stay inside these ranges and needn't reach their ends.
There are 2 independent parts, one for each index of `slides`. The reference program is written for one: setup_inputs(seed, part) draws one part's arguments, and reference() takes and returns one part's arrays. A program takes and returns all parts, laid end to end along the dimension named above; an argument that names none is the same for every part. Nothing has to cross between parts.
Inputs may be any that keep to these rules, and one draw needn't show every extreme that they name: The first block of 64 tiles of every device's 128 tiles is tissue.
All inputs are finite; a program needn't handle non-finite values.
Results may differ from the reference program's by a relative error of at most 0.024.
Values may be sent and summed in bfloat16 or wider, within the bound.
A program may use at most 64 MiB of HBM per device.

```python
import jax
import jax.numpy as jnp
from jax import lax

D = 768
H = 12
TILES_PER_CHIP = 128
DILATION_STEP = 4
GROUP = 4
BLOCK = 64
TOKENS = 2048
N_ROW = 4
N_COL = 4


def query_key_pair(key):
    base_key = jax.random.fold_in(key, 11)
    query_base = jnp.clip(jax.random.normal(jax.random.fold_in(base_key, 1), (TOKENS, D), jnp.float32), -6.0, 6.0)
    key_base = jnp.clip(jax.random.normal(jax.random.fold_in(base_key, 2), (TOKENS, D), jnp.float32), -6.0, 6.0)
    return (query_base, key_base)


def draw_query_rows(key, part):
    return query_key_pair(key)[0].astype(jnp.bfloat16)


def draw_key_rows(key, part):
    return query_key_pair(key)[1].astype(jnp.bfloat16)


def draw_tissue(key, part):
    device_count = TOKENS // TILES_PER_CHIP
    blocks_dev = TILES_PER_CHIP // BLOCK
    live_level = jax.random.randint(jax.random.fold_in(key, 21), (device_count, 1), 1, 5)
    block_rolls = jax.random.randint(jax.random.fold_in(key, 22), (device_count, blocks_dev), 0, 4)
    alive_blocks = (block_rolls < live_level).astype(jnp.int32)
    first_block = (jnp.arange(blocks_dev) == 0)[None, :]
    return jnp.where(first_block, 1, alive_blocks).reshape(-1).astype(jnp.int32)


def with_spikes(drawn, own_key, source, target, blocks, factor):
    owner, partner = [(jnp.arange(drawn.shape[axis_at]) // (drawn.shape[axis_at] // blocks)).reshape([-1 if axis == axis_at else 1 for axis in range(drawn.ndim)]) for axis_at in (source, target)]
    chosen = jax.random.permutation(own_key, blocks)[partner]
    strong = (owner == chosen) | (owner == (partner + blocks // 2) % blocks)
    return jnp.where(strong, factor * drawn, drawn)


def block_levels(own_key, extent, split, least, largest):
    level, own = 1.0, jax.random.fold_in(own_key, 6)
    for dim, blocks in split:
        heights = jnp.exp(jax.random.uniform(jax.random.fold_in(own, dim), (blocks,), jnp.float32, least / len(split), largest / len(split)))
        level = level * jnp.repeat(heights, extent[dim] // blocks).reshape([-1 if axis == dim else 1 for axis in range(len(extent))])
    return level


def gaussian(stream_key, dims, width, most, cuts=(), held_as=jnp.bfloat16):
    drawn = width * jax.random.normal(stream_key, dims, jnp.float32)
    if cuts:
        drawn = drawn * block_levels(stream_key, dims, cuts, -0.22, 0.18)
    return jnp.clip(drawn, -most, most).astype(held_as)


def gaussian_with(stream_key, dims, spread, reach, split, heavy, kind=jnp.bfloat16):
    values = spread * jax.random.normal(stream_key, dims, jnp.float32)
    if split:
        values = values * block_levels(stream_key, dims, split, -0.22, 0.18)
    return jnp.clip(with_spikes(values, jax.random.fold_in(stream_key, 3), *heavy), -reach, reach).astype(kind)


def setup_inputs(seed: int = 0, part: int = 0) -> dict:
    streams_of = jax.random.split(jax.random.key(seed), 7)
    part_splits = jax.random.split(jax.random.fold_in(streams_of[6], part), 7)
    query_rows = draw_query_rows(jax.random.fold_in(jax.random.fold_in(streams_of[6], part), 71), part)
    key_rows = draw_key_rows(jax.random.fold_in(jax.random.fold_in(streams_of[6], part), 71), part)
    value_rows = gaussian(part_splits[2], (TOKENS, D), 1.0, 6.0, ((0, 16),))
    out_grad = gaussian_with(part_splits[3], (TOKENS, D), 1.0, 6.0, ((0, 16),), (0, 1, 16, 2.0))
    tissue = draw_tissue(jax.random.fold_in(jax.random.fold_in(streams_of[6], part), 71), part)
    w_out = gaussian(streams_of[5], (D, D), D ** -0.5, 0.21875)
    return dict(query_rows=query_rows, key_rows=key_rows, value_rows=value_rows, out_grad=out_grad, tissue=tissue, w_out=w_out)


NEG_FILL = -1e30


def apply_dilation(input_array):
    head_number = input_array.shape[1]
    divide_rows = input_array.reshape((input_array.shape[0] // DILATION_STEP, DILATION_STEP) + input_array.shape[1:])
    return jnp.stack([divide_rows[:, head_index % DILATION_STEP, head_index] for head_index in range(head_number)], axis=1)


def undilate(input_array, fill_value):
    head_number = input_array.shape[1]
    selected_rows = jnp.arange(DILATION_STEP)[:, None] == (jnp.arange(head_number) % DILATION_STEP)[None, :]
    selected_rows = selected_rows.reshape((1, DILATION_STEP, head_number) + (1,) * (input_array.ndim - 2))
    scatter_back = jnp.where(selected_rows, input_array[:, None], jnp.asarray(fill_value, input_array.dtype))
    return scatter_back.reshape((input_array.shape[0] * DILATION_STEP,) + input_array.shape[1:])


def product(form, left, right):
    return jnp.einsum(form, left.astype(jnp.float32), right.astype(jnp.float32))


def masked_scores(queries, keys_in, key_live, scale_multiplier):
    raw_scores = product('qhd,khd->hqk', queries, keys_in) * scale_multiplier
    return jnp.where(key_live.T[:, None, :] > 0, raw_scores, NEG_FILL)


def forward_rows(queries, query_live, band_keys, band_values, band_live, strip_keys, strip_values, strip_live, scale_multiplier):
    scores_band = masked_scores(queries, band_keys, band_live, scale_multiplier)
    scores_strip = masked_scores(apply_dilation(queries), strip_keys, strip_live, scale_multiplier)
    top_rows = jnp.maximum(scores_band.max(-1).T, undilate(scores_strip.max(-1).T, NEG_FILL))
    total_band = jnp.sum(jnp.exp(scores_band - top_rows.T[:, :, None]), -1).T
    total_strip = jnp.sum(jnp.exp(scores_strip - apply_dilation(top_rows).T[:, :, None]), -1).T
    logsum_total = top_rows + jnp.log(total_band + undilate(total_strip, 0.0))
    weights_band = jnp.exp(scores_band - logsum_total.T[:, :, None]).astype(jnp.bfloat16)
    weights_strip = jnp.exp(scores_strip - apply_dilation(logsum_total).T[:, :, None]).astype(jnp.bfloat16)
    combined = product('hqk,khd->qhd', weights_band, band_values)
    combined = combined + undilate(product('hqk,khd->qhd', weights_strip, strip_values), 0.0)
    return (combined * query_live[:, None, None]).astype(jnp.bfloat16), logsum_total


def query_branch(queries, grads, lse_rows, dot_rows, keys_in, values_in, key_live, scale_multiplier):
    scores = masked_scores(queries, keys_in, key_live, scale_multiplier)
    probs = jnp.exp(scores - lse_rows.T[:, :, None])
    dprobs = product('qhd,khd->hqk', grads, values_in)
    dscores = (probs * (dprobs - dot_rows.T[:, :, None])).astype(jnp.bfloat16)
    return product('hqk,khd->qhd', dscores, keys_in)


def query_grads(queries, grads, lse_rows, dot_rows, band_keys, band_values, band_live, strip_keys, strip_values, strip_live, scale_multiplier):
    first_part = query_branch(queries, grads, lse_rows, dot_rows, band_keys, band_values, band_live, scale_multiplier)
    second_part = query_branch(apply_dilation(queries), apply_dilation(grads), apply_dilation(lse_rows), apply_dilation(dot_rows), strip_keys, strip_values, strip_live, scale_multiplier)
    return ((first_part + undilate(second_part, 0.0)) * scale_multiplier).astype(jnp.bfloat16)


def key_branch(keys_in, values_in, key_live, queries, grads, lse_rows, dot_rows, scale_multiplier):
    scores = masked_scores(queries, keys_in, key_live, scale_multiplier)
    probs = jnp.exp(scores - lse_rows.T[:, :, None])
    dprobs = product('qhd,khd->hqk', grads, values_in)
    dscores = (probs * (dprobs - dot_rows.T[:, :, None])).astype(jnp.bfloat16)
    key_part = product('hqk,qhd->khd', dscores, queries)
    value_part = product('hqk,qhd->khd', probs.astype(jnp.bfloat16), grads)
    return key_part, value_part


def key_grads(keys_in, values_in, key_live, band_queries, band_grads, band_lse, band_dot, strip_queries, strip_grads, strip_lse, strip_dot, scale_multiplier):
    key_one, value_one = key_branch(keys_in, values_in, key_live, band_queries, band_grads, band_lse, band_dot, scale_multiplier)
    key_two, value_two = key_branch(apply_dilation(keys_in), apply_dilation(values_in), apply_dilation(key_live), strip_queries, strip_grads, strip_lse, strip_dot, scale_multiplier)
    key_total = ((key_one + undilate(key_two, 0.0)) * scale_multiplier).astype(jnp.bfloat16)
    value_total = (value_one + undilate(value_two, 0.0)).astype(jnp.bfloat16)
    return key_total, value_total


def reference(query_rows, key_rows, value_rows, out_grad, tissue, w_out):
    head_dim = D // H
    scale_multiplier = head_dim ** -0.5
    dilated_tiles = TILES_PER_CHIP // DILATION_STEP
    live_tiles = jnp.repeat(tissue, BLOCK).astype(jnp.float32)
    alive_per_head = jnp.broadcast_to(live_tiles[:, None], (TOKENS, H))

    def blocks(input_array):
        return input_array.reshape((N_ROW, N_COL, TILES_PER_CHIP) + input_array.shape[1:])

    def dilated_block_set(input_array):
        return apply_dilation(input_array).reshape((N_ROW, N_COL, dilated_tiles) + input_array.shape[1:])

    query_per_head = query_rows.reshape(TOKENS, H, head_dim)
    key_per_head = key_rows.reshape(TOKENS, H, head_dim)
    value_per_head = value_rows.reshape(TOKENS, H, head_dim)
    query_blk, key_blk, value_blk = blocks(query_per_head), blocks(key_per_head), blocks(value_per_head)
    live_blk = blocks(alive_per_head)
    query_live_blk = live_tiles.reshape(N_ROW, N_COL, TILES_PER_CHIP)
    dilated_keys, dilated_values, dilated_alive = dilated_block_set(key_per_head), dilated_block_set(value_per_head), dilated_block_set(alive_per_head)

    def band(input_array, row_pos, column_place):
        start_row = (row_pos // GROUP) * GROUP
        column_part = jnp.take(input_array, column_place, axis=1)
        picked = lax.dynamic_slice_in_dim(column_part, start_row, GROUP, 0)
        return picked.reshape((GROUP * TILES_PER_CHIP,) + input_array.shape[3:])

    def strip_window(input_array, column_place):
        return jnp.take(input_array, column_place, axis=1).reshape((-1,) + input_array.shape[3:])

    def forward_dev(dev_index):
        row_pos = dev_index // N_COL
        column_place = dev_index % N_COL
        return forward_rows(query_blk[row_pos, column_place], query_live_blk[row_pos, column_place],
                            band(key_blk, row_pos, column_place), band(value_blk, row_pos, column_place), band(live_blk, row_pos, column_place),
                            strip_window(dilated_keys, column_place), strip_window(dilated_values, column_place), strip_window(dilated_alive, column_place), scale_multiplier)

    dev_list = jnp.arange(N_ROW * N_COL, dtype=jnp.int32)
    attended, logsum_total = lax.map(forward_dev, dev_list)
    attended_rows = attended.reshape(TOKENS, D)
    logsum_total = logsum_total.reshape(TOKENS, H)
    output = jnp.dot(attended_rows, w_out, preferred_element_type=jnp.float32).astype(jnp.bfloat16)
    grad_rows = (jnp.dot(out_grad, w_out.T, preferred_element_type=jnp.float32) * live_tiles[:, None]).astype(jnp.bfloat16)
    gradient_per_head = grad_rows.reshape(TOKENS, H, head_dim)
    score_gradient = jnp.sum(gradient_per_head.astype(jnp.float32) * attended_rows.reshape(TOKENS, H, head_dim).astype(jnp.float32), -1)
    weight_grad = jnp.dot(attended_rows.T, out_grad, preferred_element_type=jnp.float32)
    grad_blk, lse_blk, dot_blk = blocks(gradient_per_head), blocks(logsum_total), blocks(score_gradient)
    dilated_queries, dilated_gradient = dilated_block_set(query_per_head), dilated_block_set(gradient_per_head)
    dilated_logsumexp, dilated_scores = dilated_block_set(logsum_total), dilated_block_set(score_gradient)

    def backward_dev(dev_index):
        row_pos = dev_index // N_COL
        column_place = dev_index % N_COL
        query_part = query_grads(query_blk[row_pos, column_place], grad_blk[row_pos, column_place], lse_blk[row_pos, column_place], dot_blk[row_pos, column_place],
                                 band(key_blk, row_pos, column_place), band(value_blk, row_pos, column_place), band(live_blk, row_pos, column_place),
                                 strip_window(dilated_keys, column_place), strip_window(dilated_values, column_place), strip_window(dilated_alive, column_place), scale_multiplier)
        key_part, value_part = key_grads(key_blk[row_pos, column_place], value_blk[row_pos, column_place], live_blk[row_pos, column_place],
                                         band(query_blk, row_pos, column_place), band(grad_blk, row_pos, column_place),
                                         band(lse_blk, row_pos, column_place), band(dot_blk, row_pos, column_place),
                                         strip_window(dilated_queries, column_place), strip_window(dilated_gradient, column_place),
                                         strip_window(dilated_logsumexp, column_place), strip_window(dilated_scores, column_place), scale_multiplier)
        return query_part, key_part, value_part

    query_grad, key_grad, value_grad = lax.map(backward_dev, dev_list)
    return (output, query_grad.reshape(TOKENS, D), key_grad.reshape(TOKENS, D),
            value_grad.reshape(TOKENS, D), weight_grad)
```

```python
import functools

import jax
import jax.numpy as jnp
from jax import lax
from jax.experimental import pallas as pl
from jax.experimental.pallas import tpu as pltpu
from jax.sharding import PartitionSpec as P

H = 12
DILATION_STEP = 4
GROUP = 4
BLOCK = 64


NEG_FILL = -1e30


def from_behind(array, axis, by):
    devices = lax.axis_size(axis)
    pairs = [(i, i + by) for i in range(devices) if 0 <= i + by < devices]
    return lax.ppermute(array, axis, pairs)


def apply_dilation(input_array):
    head_number = input_array.shape[1]
    divide_rows = input_array.reshape(
        (input_array.shape[0] // DILATION_STEP, DILATION_STEP) + input_array.shape[1:]
    )
    return jnp.stack(
        [
            divide_rows[:, head_index % DILATION_STEP, head_index]
            for head_index in range(head_number)
        ],
        axis=1,
    )


def undilate(input_array, fill_value):
    head_number = input_array.shape[1]
    selected_rows = (
        jnp.arange(DILATION_STEP)[:, None] == (jnp.arange(head_number) % DILATION_STEP)[None, :]
    )
    selected_rows = selected_rows.reshape(
        (1, DILATION_STEP, head_number) + (1,) * (input_array.ndim - 2)
    )
    scatter_back = jnp.where(
        selected_rows, input_array[:, None], jnp.asarray(fill_value, input_array.dtype)
    )
    return scatter_back.reshape((input_array.shape[0] * DILATION_STEP,) + input_array.shape[1:])


def product(form, left, right):
    return jnp.einsum(form, left, right, preferred_element_type=jnp.float32)


def masked_scores(queries, keys_in, key_live, scale_multiplier):
    raw_scores = product("qhd,khd->hqk", queries, keys_in) * scale_multiplier
    return jnp.where(key_live.T[:, None, :] > 0, raw_scores, NEG_FILL)


def forward_rows(
    queries,
    query_live,
    band_keys,
    band_values,
    band_live,
    strip_keys,
    strip_values,
    strip_live,
    scale_multiplier,
):
    scores_band = masked_scores(queries, band_keys, band_live, scale_multiplier)
    scores_strip = masked_scores(apply_dilation(queries), strip_keys, strip_live, scale_multiplier)
    top_rows = jnp.maximum(scores_band.max(-1).T, undilate(scores_strip.max(-1).T, NEG_FILL))
    total_band = jnp.sum(jnp.exp(scores_band - top_rows.T[:, :, None]), -1).T
    total_strip = jnp.sum(jnp.exp(scores_strip - apply_dilation(top_rows).T[:, :, None]), -1).T
    logsum_total = top_rows + jnp.log(total_band + undilate(total_strip, 0.0))
    weights_band = jnp.exp(scores_band - logsum_total.T[:, :, None]).astype(jnp.bfloat16)
    weights_strip = jnp.exp(scores_strip - apply_dilation(logsum_total).T[:, :, None]).astype(
        jnp.bfloat16
    )
    combined = product("hqk,khd->qhd", weights_band, band_values)
    combined = combined + undilate(product("hqk,khd->qhd", weights_strip, strip_values), 0.0)
    return ((combined * query_live[:, None, None]).astype(jnp.bfloat16), logsum_total)


def query_branch(
    queries, grads, lse_rows, dot_rows, keys_in, values_in, key_live, scale_multiplier
):
    scores = masked_scores(queries, keys_in, key_live, scale_multiplier)
    probs = jnp.exp(scores - lse_rows.T[:, :, None])
    dprobs = product("qhd,khd->hqk", grads, values_in)
    dscores = (probs * (dprobs - dot_rows.T[:, :, None])).astype(jnp.bfloat16)
    return product("hqk,khd->qhd", dscores, keys_in)


def query_grads(
    queries,
    grads,
    lse_rows,
    dot_rows,
    band_keys,
    band_values,
    band_live,
    strip_keys,
    strip_values,
    strip_live,
    scale_multiplier,
):
    first_part = query_branch(
        queries, grads, lse_rows, dot_rows, band_keys, band_values, band_live, scale_multiplier
    )
    second_part = query_branch(
        apply_dilation(queries),
        apply_dilation(grads),
        apply_dilation(lse_rows),
        apply_dilation(dot_rows),
        strip_keys,
        strip_values,
        strip_live,
        scale_multiplier,
    )
    return ((first_part + undilate(second_part, 0.0)) * scale_multiplier).astype(jnp.bfloat16)


def key_branch(keys_in, values_in, key_live, queries, grads, lse_rows, dot_rows, scale_multiplier):
    scores = masked_scores(queries, keys_in, key_live, scale_multiplier)
    probs = jnp.exp(scores - lse_rows.T[:, :, None])
    dprobs = product("qhd,khd->hqk", grads, values_in)
    dscores = (probs * (dprobs - dot_rows.T[:, :, None])).astype(jnp.bfloat16)
    key_part = product("hqk,qhd->khd", dscores, queries)
    value_part = product("hqk,qhd->khd", probs.astype(jnp.bfloat16), grads)
    return (key_part, value_part)


def key_grads(
    keys_in,
    values_in,
    key_live,
    band_queries,
    band_grads,
    band_lse,
    band_dot,
    strip_queries,
    strip_grads,
    strip_lse,
    strip_dot,
    scale_multiplier,
):
    key_one, value_one = key_branch(
        keys_in, values_in, key_live, band_queries, band_grads, band_lse, band_dot, scale_multiplier
    )
    key_two, value_two = key_branch(
        apply_dilation(keys_in),
        apply_dilation(values_in),
        apply_dilation(key_live),
        strip_queries,
        strip_grads,
        strip_lse,
        strip_dot,
        scale_multiplier,
    )
    key_total = ((key_one + undilate(key_two, 0.0)) * scale_multiplier).astype(jnp.bfloat16)
    value_total = (value_one + undilate(value_two, 0.0)).astype(jnp.bfloat16)
    return (key_total, value_total)


def pick_members(stacked, pieces, offsets, group_pos):
    members = []
    for member in range(GROUP):
        piece = stacked
        for offset in offsets:
            piece = jnp.where(group_pos - member == offset, pieces[offset], piece)
        members.append(piece)
    return jnp.concatenate(members, 1)


def fetch_rows(stacked, row_index):
    group_pos = row_index % GROUP
    offsets = [offset for offset in range(1 - GROUP, GROUP) if offset != 0]
    pieces = {}
    for offset in offsets:
        pieces[offset] = from_behind(stacked, "row", offset)
    return pick_members(stacked, pieces, offsets, group_pos)


def fetch_stats(stacked, row_index):
    group_pos = row_index % GROUP
    offsets = [offset for offset in range(1 - GROUP, GROUP) if offset != 0]
    pieces = {}
    for offset in offsets:
        pieces[offset] = from_behind(stacked, "row", offset)
    return pick_members(stacked, pieces, offsets, group_pos)


def gather_strip(stacked):
    return lax.all_gather(stacked, "row", axis=1, tiled=True)


def shards(query_rows, key_rows, value_rows, out_grad, tissue, w_out):
    row_count, width = query_rows.shape
    head_dim = width // H
    scale_multiplier = head_dim ** (-0.5)
    row_devs = lax.axis_size("row")
    col_devs = lax.axis_size("col")
    row_index = lax.axis_index("row")
    col_index = lax.axis_index("col")
    blocks_dev = row_count // BLOCK
    device_pos = row_index * col_devs + col_index
    own_live = jnp.repeat(
        lax.dynamic_slice_in_dim(tissue, device_pos * blocks_dev, blocks_dev, 0), BLOCK
    ).astype(jnp.float32)
    column_flags = jnp.take(tissue.reshape(row_devs, col_devs, blocks_dev), col_index, axis=1)
    group_first = row_index // GROUP * GROUP
    band_blocks = lax.dynamic_slice_in_dim(column_flags, group_first, GROUP, 0).reshape(-1)
    band_flags = jnp.repeat(band_blocks, BLOCK).astype(jnp.float32)
    band_live = jnp.broadcast_to(band_flags[:, None], (GROUP * row_count, H))
    strip_flags = jnp.repeat(column_flags.reshape(-1), BLOCK).astype(jnp.float32)
    strip_live = apply_dilation(jnp.broadcast_to(strip_flags[:, None], (row_devs * row_count, H)))
    own_heads = jnp.broadcast_to(own_live[:, None], (row_count, H))
    query_per_head = query_rows.reshape(row_count, H, head_dim)
    key_per_head = key_rows.reshape(row_count, H, head_dim)
    value_per_head = value_rows.reshape(row_count, H, head_dim)
    band_pair = fetch_rows(jnp.stack([key_rows, value_rows]), row_index)
    band_keys = band_pair[0].reshape(-1, H, head_dim)
    band_values = band_pair[1].reshape(-1, H, head_dim)
    strip_pair = gather_strip(
        jnp.stack(
            [
                apply_dilation(key_per_head).reshape(-1, width),
                apply_dilation(value_per_head).reshape(-1, width),
            ]
        )
    )
    strip_keys = strip_pair[0].reshape(-1, H, head_dim)
    strip_values = strip_pair[1].reshape(-1, H, head_dim)
    attended, logsum_total = forward_rows(
        query_per_head,
        own_live,
        band_keys,
        band_values,
        band_live,
        strip_keys,
        strip_values,
        strip_live,
        scale_multiplier,
    )
    attended_rows = attended.reshape(row_count, width)
    output = jnp.dot(attended_rows, w_out, preferred_element_type=jnp.float32).astype(jnp.bfloat16)
    grad_rows = (
        jnp.dot(out_grad, w_out.T, preferred_element_type=jnp.float32) * own_live[:, None]
    ).astype(jnp.bfloat16)
    gradient_per_head = grad_rows.reshape(row_count, H, head_dim)
    score_gradient = jnp.einsum(
        "qhd,qhd->qh", gradient_per_head, attended, preferred_element_type=jnp.float32
    )
    weight_term = jnp.dot(attended_rows.T, out_grad, preferred_element_type=jnp.float32)
    weight_share = lax.psum_scatter(weight_term, "row", scatter_dimension=1, tiled=True)
    weight_grad = lax.psum(weight_share, "col")
    band_query_pair = fetch_rows(jnp.stack([query_rows, grad_rows]), row_index)
    band_stat_pair = fetch_stats(jnp.stack([logsum_total, score_gradient]), row_index)
    strip_query_pair = gather_strip(
        jnp.stack(
            [
                apply_dilation(query_per_head).reshape(-1, width),
                apply_dilation(gradient_per_head).reshape(-1, width),
            ]
        )
    )
    strip_stat_pair = lax.all_gather(
        jnp.stack([apply_dilation(logsum_total), apply_dilation(score_gradient)]),
        "row",
        axis=1,
        tiled=True,
    )
    query_grad = query_grads(
        query_per_head,
        gradient_per_head,
        logsum_total,
        score_gradient,
        band_keys,
        band_values,
        band_live,
        strip_keys,
        strip_values,
        strip_live,
        scale_multiplier,
    )
    key_grad, value_grad = key_grads(
        key_per_head,
        value_per_head,
        own_heads,
        band_query_pair[0].reshape(-1, H, head_dim),
        band_query_pair[1].reshape(-1, H, head_dim),
        band_stat_pair[0],
        band_stat_pair[1],
        strip_query_pair[0].reshape(-1, H, head_dim),
        strip_query_pair[1].reshape(-1, H, head_dim),
        strip_stat_pair[0],
        strip_stat_pair[1],
        scale_multiplier,
    )
    return (
        output,
        query_grad.reshape(row_count, width),
        key_grad.reshape(row_count, width),
        value_grad.reshape(row_count, width),
        weight_grad,
    )


MESH = pl.DeviceIdType.MESH
F32 = jnp.float32
BF16 = jnp.bfloat16


def dot_nn(a, b):
    return lax.dot_general(a, b, (((1,), (0,)), ((), ())), preferred_element_type=F32)


def dot_nt(a, b):
    return lax.dot_general(a, b, (((1,), (1,)), ((), ())), preferred_element_type=F32)


def dot_tn(a, b):
    return lax.dot_general(a, b, (((0,), (0,)), ((), ())), preferred_element_type=F32)


def column_kernel(
    R, C, HP, HD, N,
    tissue_hbm, q_hbm, k_hbm, v_hbm, og_hbm, w_hbm,
    out_ref, dq_ref, dk_ref, dv_ref, wg_ref,
    tissue_ref, q_ref, k_ref, v_ref, w_ref, wfull, load_sem,
    tx, rx, ogx, otx, orx, gtx, grx, w1tx, w1rx, w2tx, w2rx, w3rx,
    kbias, probs, dsc, gt,
    a_send, a_recv, og_send, og_recv, o_send, o_recv, g_send, g_recv,
    w1_send, w1_recv, w2_send, w2_recv, w3_send, w3_recv,
):
    T = R * N
    HW = HP * HD
    WIN = w1tx.shape[-1]
    WQ = HW // C
    me = lax.axis_index("row")
    col = lax.axis_index("col")
    scale = HD ** (-0.5)

    def row_dev(i):
        return {"row": i}

    def col_dev(i):
        return {"col": i}

    loads = [
        pltpu.make_async_copy(src, dst, load_sem.at[n])
        for n, (src, dst) in enumerate((
            (og_hbm, ogx.at[me]), (q_hbm, q_ref), (k_hbm, k_ref), (v_hbm, v_ref),
            (tissue_hbm, tissue_ref), (w_hbm, w_ref),
        ))
    ]
    for load in loads:
        load.start()

    barrier = pltpu.get_barrier_semaphore()
    for d in range(1, R):
        pl.semaphore_signal(
            barrier, inc=1, device_id=row_dev(lax.rem(me + d, R)), device_id_type=MESH
        )
    for d in range(1, C):
        pl.semaphore_signal(
            barrier, inc=1, device_id=col_dev(lax.rem(col + d, C)), device_id_type=MESH
        )

    def row_copy(src, dst, send, recv, to):
        return pltpu.make_async_remote_copy(
            src_ref=src, dst_ref=dst, send_sem=send, recv_sem=recv,
            device_id=row_dev(to), device_id_type=MESH,
        )

    def col_copy(src, dst, send, recv, to):
        return pltpu.make_async_remote_copy(
            src_ref=src, dst_ref=dst, send_sem=send, recv_sem=recv,
            device_id=col_dev(to), device_id_type=MESH,
        )

    def og_copy(shard, side, hop, to):
        return row_copy(
            ogx.at[shard], ogx.at[shard], og_send.at[side, hop], og_recv.at[shard], to
        )

    partners = (R - 1 - me, lax.rem(me + R // 2, R), me + 1 - 2 * lax.rem(me, 2))
    partners = tuple(enumerate(partners))

    loads[0].wait()
    pl.semaphore_wait(barrier, R - 1 + C - 1)

    @pl.when(me + 1 < R)
    def _():
        og_copy(me, 0, 0, me + 1).start()

    @pl.when(me >= 1)
    def _():
        og_copy(me, 1, 0, me - 1).start()

    for a, ref in enumerate((q_ref, k_ref, v_ref)):
        loads[a + 1].wait()
        value = ref[...].astype(F32)
        if a == 0:
            value = value * scale
        value = value.T.astype(BF16)
        for d in range(R):
            for i in range(HP):
                start = (d * HP + i) * HD
                tx[d, i, a] = value[start : start + HD]

    pending = []

    def send_head(i):
        for d, to in partners:
            copy = row_copy(tx.at[to, i], rx.at[me, i], a_send.at[i, d], a_recv.at[i, d], to)
            copy.start()
            pending.append(copy)

    def og_arrive(j):
        @pl.when(me - j >= 0)
        def _():
            og_copy(me - j, 0, j, me).wait_recv()

        if j < R - 1:
            @pl.when((me - j >= 0) & (me + 1 < R))
            def _():
                og_copy(me - j, 0, j, me + 1).start()

        @pl.when(me + j < R)
        def _():
            og_copy(me + j, 1, j, me).wait_recv()

        if j < R - 1:
            @pl.when((me + j < R) & (me >= 1))
            def _():
                og_copy(me + j, 1, j, me - 1).start()

    send_head(0)
    loads[4].wait()
    rx[me] = tx[me]

    QC = kbias.shape[1]
    lane = lax.broadcasted_iota(jnp.int32, (1, T), 1)
    qlive = jnp.zeros((1, T), F32)
    per_dev = N // BLOCK
    for s in range(R):
        for b in range(per_dev):
            flag = tissue_ref[(s * C + col) * per_dev + b].astype(F32)
            j = s * per_dev + b
            kbias[j * BLOCK : (j + 1) * BLOCK, :] = jnp.full((BLOCK, QC), (1.0 - flag) * NEG_FILL, F32)
            qlive = jnp.where(lane // BLOCK == j, flag, qlive)

    og_arrive(1)
    for i in range(1, HP):
        send_head(i)

    krow = lax.broadcasted_iota(jnp.int32, (T, QC), 0) % DILATION_STEP
    qlane = lax.broadcasted_iota(jnp.int32, (T, QC), 1) % DILATION_STEP

    def gathered(i, a):
        return jnp.concatenate([rx[s, i, a] for s in range(R)], axis=1)

    attended = []
    for i in range(HP):
        for d, src in partners:
            row_copy(tx.at[src, i], rx.at[src, i], a_send.at[i, d], a_recv.at[i, d], src).wait_recv()
        offset = (me * HP + i) % DILATION_STEP
        twice = jnp.where((krow == offset) & (qlane == offset), 2.0, 1.0)
        qt, kt, vt = gathered(i, 0), gathered(i, 1), gathered(i, 2)
        parts = []
        for c in range(T // QC):
            cols = slice(c * QC, (c + 1) * QC)
            s = dot_tn(kt, qt[:, cols]) + kbias[...]
            top = jnp.max(s, axis=0, keepdims=True)
            p = jnp.exp(s - top) * twice
            total = jnp.sum(p, axis=0, keepdims=True)
            pb = (p * (1.0 / total)).astype(BF16)
            probs[i, :, cols] = pb
            parts.append(dot_nn(vt, pb) * qlive[:, cols])
        o = jnp.concatenate(parts, axis=1).astype(BF16)
        attended.append(o)
        for d in range(R):
            otx[d, i] = o[:, d * N : (d + 1) * N]
        for d, to in partners:
            copy = row_copy(otx.at[to, i], orx.at[me, i], o_send.at[i, d], o_recv.at[i, d], to)
            copy.start()
            pending.append(copy)
        orx[me, i] = otx[me, i]
        if i == 0:
            og_arrive(2)
    for j in range(3, R):
        og_arrive(j)
    loads[5].wait()

    o_all = jnp.concatenate(attended, axis=0)
    og_all = ogx[...].reshape(T, R * HW)
    for r in range(R):
        first = r * HW // 128 * 128
        term = dot_nn(o_all, og_all[:, first : first + WIN]).astype(BF16)
        for c in range(C):
            w1tx[c, r] = term[c * WQ : (c + 1) * WQ]
    for d in range(1, C):
        to = lax.rem(col + d, C)
        copy = col_copy(w1tx.at[to], w1rx.at[col], w1_send.at[d], w1_recv.at[col], to)
        copy.start()
        pending.append(copy)
    w_mine = w_ref[pl.ds(pl.multiple_of(me * HW, HW), HW), :]
    gt[...] = (dot_nt(w_mine, og_all) * qlive).astype(BF16)

    for i in range(HP):
        qt, kt, vt = gathered(i, 0), gathered(i, 1), gathered(i, 2)
        g = gt[i * HD : (i + 1) * HD, :]
        dots = jnp.sum(g.astype(F32) * attended[i].astype(F32), axis=0, keepdims=True)
        parts = []
        for c in range(T // QC):
            cols = slice(c * QC, (c + 1) * QC)
            dp = dot_tn(vt, g[:, cols])
            ds = (probs[i, :, cols].astype(F32) * (dp - dots[:, cols])).astype(BF16)
            dsc[:, cols] = ds
            parts.append(dot_nn(kt, ds) * scale)
        results = (
            jnp.concatenate(parts, axis=1),
            dot_nt(qt, dsc[...]),
            dot_nt(g, probs[i]),
        )
        for a, value in enumerate(results):
            value = value.astype(BF16)
            for d in range(R):
                gtx[d, i, a] = value[:, d * N : (d + 1) * N]
        for d, to in partners:
            copy = row_copy(gtx.at[to, i], grx.at[me, i], g_send.at[i, d], g_recv.at[i, d], to)
            copy.start()
            pending.append(copy)
        grx[me, i] = gtx[me, i]
        if i == 0:
            w1rx[col] = w1tx[col]
            for d in range(1, C):
                src = lax.rem(col + d, C)
                col_copy(w1tx.at[src], w1rx.at[src], w1_send.at[d], w1_recv.at[src], src).wait_recv()
            share = w1rx[0].astype(F32)
            for c in range(1, C):
                share = share + w1rx[c].astype(F32)
            w2tx[...] = share.astype(BF16)
            for d in range(1, R):
                to = lax.rem(me + d, R)
                copy = row_copy(w2tx.at[to], w2rx.at[me], w2_send.at[d], w2_recv.at[me], to)
                copy.start()
                pending.append(copy)
            w2rx[me] = w2tx[me]
        if i == HP - 1:
            for d in range(1, R):
                src = lax.rem(me + d, R)
                row_copy(w2tx.at[src], w2rx.at[src], w2_send.at[d], w2_recv.at[src], src).wait_recv()
            for d in range(1, C):
                to = lax.rem(col + d, C)
                copy = col_copy(w2rx, w3rx.at[col], w3_send.at[d], w3_recv.at[col], to)
                copy.start()
                pending.append(copy)
            w3rx[col] = w2rx[...]

    for i in range(HP):
        for d, src in partners:
            row_copy(otx.at[src, i], orx.at[src, i], o_send.at[i, d], o_recv.at[i, d], src).wait_recv()
    out_ref[...] = dot_tn(orx[...].reshape(R * HW, N), w_ref[...]).astype(BF16)
    for d in range(1, C):
        src = lax.rem(col + d, C)
        col_copy(w2rx, w3rx.at[src], w3_send.at[d], w3_recv.at[src], src).wait_recv()
    odd = (me * HW) % 128 != 0
    for c in range(C):
        for s in range(R):
            piece = w3rx[c, s].astype(F32)
            piece = jnp.where(odd, pltpu.roll(piece, WIN - (HW % 128), 1), piece)
            start = s * HW + c * WQ
            wfull[start : start + WQ, :] = piece
    wg_ref[...] = wfull[...].T[:HW]
    for i in range(HP):
        for d, src in partners:
            row_copy(gtx.at[src, i], grx.at[src, i], g_send.at[i, d], g_recv.at[i, d], src).wait_recv()
    for a, ref in enumerate((dq_ref, dk_ref, dv_ref)):
        value = jnp.concatenate([grx[s, i, a] for s in range(R) for i in range(HP)], axis=0)
        ref[...] = value.astype(F32).T.astype(BF16)

    for copy in pending:
        copy.wait_send()
    for j in range(R - 1):
        @pl.when((me - j >= 0) & (me + 1 < R))
        def _():
            og_copy(me - j, 0, j, me + 1).wait_send()

        @pl.when((me + j < R) & (me >= 1))
        def _():
            og_copy(me + j, 1, j, me - 1).wait_send()


def write_kernel(*refs):
    held, outs, store_sem = refs[:5], refs[5:10], refs[10]
    stores = [pltpu.make_async_copy(held[n], outs[n], store_sem.at[n]) for n in range(5)]
    for store in stores:
        store.start()
    for store in stores:
        store.wait()


def column_shards(query_rows, key_rows, value_rows, out_grad, tissue, w_out):
    N, width = query_rows.shape
    R = lax.axis_size("row")
    C = lax.axis_size("col")
    HP = H // R
    HD = width // H
    HW = HP * HD
    T = R * N
    WIN = -(-HW // 128) * 128
    WQ = HW // C
    QC = 256
    vmem = pl.BlockSpec(memory_space=pltpu.VMEM)
    dma = pltpu.SemaphoreType.DMA
    rows = jax.ShapeDtypeStruct((N, width), BF16)
    hbm = pl.BlockSpec(memory_space=pltpu.HBM)
    shapes = (rows, rows, rows, rows, jax.ShapeDtypeStruct((HW, width), F32))
    results = pl.pallas_call(
        functools.partial(column_kernel, R, C, HP, HD, N),
        out_shape=tuple(pltpu.VMEM(s.shape, s.dtype) for s in shapes),
        in_specs=[hbm] * 6,
        out_specs=(vmem,) * 5,
        scratch_shapes=[
            pltpu.SMEM(tissue.shape, jnp.int32),
            pltpu.VMEM((N, width), BF16),
            pltpu.VMEM((N, width), BF16),
            pltpu.VMEM((N, width), BF16),
            pltpu.VMEM((width, width), BF16),
            pltpu.VMEM((width, WIN), F32),
            dma((6,)),
            pltpu.VMEM((R, HP, 3, HD, N), BF16),
            pltpu.VMEM((R, HP, 3, HD, N), BF16),
            pltpu.VMEM((R, N, width), BF16),
            pltpu.VMEM((R, HP, HD, N), BF16),
            pltpu.VMEM((R, HP, HD, N), BF16),
            pltpu.VMEM((R, HP, 3, HD, N), BF16),
            pltpu.VMEM((R, HP, 3, HD, N), BF16),
            pltpu.VMEM((C, R, WQ, WIN), BF16),
            pltpu.VMEM((C, R, WQ, WIN), BF16),
            pltpu.VMEM((R, WQ, WIN), BF16),
            pltpu.VMEM((R, WQ, WIN), BF16),
            pltpu.VMEM((C, R, WQ, WIN), BF16),
            pltpu.VMEM((T, QC), F32),
            pltpu.VMEM((HP, T, T), BF16),
            pltpu.VMEM((T, T), BF16),
            pltpu.VMEM((HW, T), BF16),
            dma((HP, R)), dma((HP, R)),
            dma((2, R)), dma((R,)),
            dma((HP, R)), dma((HP, R)),
            dma((HP, R)), dma((HP, R)),
            dma((C,)), dma((C,)),
            dma((R,)), dma((R,)),
            dma((C,)), dma((C,)),
        ],
        compiler_params=pltpu.CompilerParams(
            collective_id=0, has_side_effects=True, vmem_limit_bytes=40 * 2**20
        ),
    )(*(pltpu.with_memory_space_constraint(x, pltpu.HBM) for x in (tissue, query_rows, key_rows, value_rows, out_grad, w_out)))
    *four, weight_t = pl.pallas_call(
        write_kernel,
        out_shape=shapes,
        in_specs=[vmem] * 5,
        out_specs=(hbm,) * 5,
        scratch_shapes=[dma((5,))],
        compiler_params=pltpu.CompilerParams(vmem_limit_bytes=2**20),
    )(*(pltpu.with_memory_space_constraint(x, pltpu.VMEM) for x in results))
    return (*four, weight_t.T)


def solution(mesh):
    in_specs = (
        P(("slides", "row", "col"), None),
        P(("slides", "row", "col"), None),
        P(("slides", "row", "col"), None),
        P(("slides", "row", "col"), None),
        P("slides"),
        P(),
    )
    out_specs = (
        P(("slides", "row", "col"), None),
        P(("slides", "row", "col"), None),
        P(("slides", "row", "col"), None),
        P(("slides", "row", "col"), None),
        P("slides", "row"),
    )
    whole_column = mesh.shape["row"] == GROUP
    body = column_shards if whole_column else shards
    return jax.shard_map(body, mesh=mesh, in_specs=in_specs, out_specs=out_specs, check_vma=False)
```

```python
import functools
import math

import jax
import jax.numpy as jnp
from jax import lax
from jax.experimental import pallas as pl
from jax.experimental.pallas import tpu as pltpu
from jax.sharding import PartitionSpec as P

H = 12
DILATION_STEP = 4
GROUP = 4
BLOCK = 64


NEG_FILL = -1e30


def from_behind(array, axis, by):
    devices = lax.axis_size(axis)
    pairs = [(i, i + by) for i in range(devices) if 0 <= i + by < devices]
    return lax.ppermute(array, axis, pairs)


def apply_dilation(input_array):
    head_number = input_array.shape[1]
    divide_rows = input_array.reshape(
        (input_array.shape[0] // DILATION_STEP, DILATION_STEP) + input_array.shape[1:]
    )
    return jnp.stack(
        [
            divide_rows[:, head_index % DILATION_STEP, head_index]
            for head_index in range(head_number)
        ],
        axis=1,
    )


def undilate(input_array, fill_value):
    head_number = input_array.shape[1]
    selected_rows = (
        jnp.arange(DILATION_STEP)[:, None] == (jnp.arange(head_number) % DILATION_STEP)[None, :]
    )
    selected_rows = selected_rows.reshape(
        (1, DILATION_STEP, head_number) + (1,) * (input_array.ndim - 2)
    )
    scatter_back = jnp.where(
        selected_rows, input_array[:, None], jnp.asarray(fill_value, input_array.dtype)
    )
    return scatter_back.reshape((input_array.shape[0] * DILATION_STEP,) + input_array.shape[1:])


def product(form, left, right):
    return jnp.einsum(form, left, right, preferred_element_type=jnp.float32)


def masked_scores(queries, keys_in, key_live, scale_multiplier):
    raw_scores = product("qhd,khd->hqk", queries, keys_in) * scale_multiplier
    return jnp.where(key_live.T[:, None, :] > 0, raw_scores, NEG_FILL)


def forward_rows(
    queries,
    query_live,
    band_keys,
    band_values,
    band_live,
    strip_keys,
    strip_values,
    strip_live,
    scale_multiplier,
):
    scores_band = masked_scores(queries, band_keys, band_live, scale_multiplier)
    scores_strip = masked_scores(apply_dilation(queries), strip_keys, strip_live, scale_multiplier)
    top_rows = jnp.maximum(scores_band.max(-1).T, undilate(scores_strip.max(-1).T, NEG_FILL))
    total_band = jnp.sum(jnp.exp(scores_band - top_rows.T[:, :, None]), -1).T
    total_strip = jnp.sum(jnp.exp(scores_strip - apply_dilation(top_rows).T[:, :, None]), -1).T
    logsum_total = top_rows + jnp.log(total_band + undilate(total_strip, 0.0))
    weights_band = jnp.exp(scores_band - logsum_total.T[:, :, None]).astype(jnp.bfloat16)
    weights_strip = jnp.exp(scores_strip - apply_dilation(logsum_total).T[:, :, None]).astype(
        jnp.bfloat16
    )
    combined = product("hqk,khd->qhd", weights_band, band_values)
    combined = combined + undilate(product("hqk,khd->qhd", weights_strip, strip_values), 0.0)
    return ((combined * query_live[:, None, None]).astype(jnp.bfloat16), logsum_total)


def query_branch(
    queries, grads, lse_rows, dot_rows, keys_in, values_in, key_live, scale_multiplier
):
    scores = masked_scores(queries, keys_in, key_live, scale_multiplier)
    probs = jnp.exp(scores - lse_rows.T[:, :, None])
    dprobs = product("qhd,khd->hqk", grads, values_in)
    dscores = (probs * (dprobs - dot_rows.T[:, :, None])).astype(jnp.bfloat16)
    return product("hqk,khd->qhd", dscores, keys_in)


def query_grads(
    queries,
    grads,
    lse_rows,
    dot_rows,
    band_keys,
    band_values,
    band_live,
    strip_keys,
    strip_values,
    strip_live,
    scale_multiplier,
):
    first_part = query_branch(
        queries, grads, lse_rows, dot_rows, band_keys, band_values, band_live, scale_multiplier
    )
    second_part = query_branch(
        apply_dilation(queries),
        apply_dilation(grads),
        apply_dilation(lse_rows),
        apply_dilation(dot_rows),
        strip_keys,
        strip_values,
        strip_live,
        scale_multiplier,
    )
    return ((first_part + undilate(second_part, 0.0)) * scale_multiplier).astype(jnp.bfloat16)


def key_branch(keys_in, values_in, key_live, queries, grads, lse_rows, dot_rows, scale_multiplier):
    scores = masked_scores(queries, keys_in, key_live, scale_multiplier)
    probs = jnp.exp(scores - lse_rows.T[:, :, None])
    dprobs = product("qhd,khd->hqk", grads, values_in)
    dscores = (probs * (dprobs - dot_rows.T[:, :, None])).astype(jnp.bfloat16)
    key_part = product("hqk,qhd->khd", dscores, queries)
    value_part = product("hqk,qhd->khd", probs.astype(jnp.bfloat16), grads)
    return (key_part, value_part)


def key_grads(
    keys_in,
    values_in,
    key_live,
    band_queries,
    band_grads,
    band_lse,
    band_dot,
    strip_queries,
    strip_grads,
    strip_lse,
    strip_dot,
    scale_multiplier,
):
    key_one, value_one = key_branch(
        keys_in, values_in, key_live, band_queries, band_grads, band_lse, band_dot, scale_multiplier
    )
    key_two, value_two = key_branch(
        apply_dilation(keys_in),
        apply_dilation(values_in),
        apply_dilation(key_live),
        strip_queries,
        strip_grads,
        strip_lse,
        strip_dot,
        scale_multiplier,
    )
    key_total = ((key_one + undilate(key_two, 0.0)) * scale_multiplier).astype(jnp.bfloat16)
    value_total = (value_one + undilate(value_two, 0.0)).astype(jnp.bfloat16)
    return (key_total, value_total)


def pick_members(stacked, pieces, offsets, group_pos):
    members = []
    for member in range(GROUP):
        piece = stacked
        for offset in offsets:
            piece = jnp.where(group_pos - member == offset, pieces[offset], piece)
        members.append(piece)
    return jnp.concatenate(members, 1)


def fetch_rows(stacked, row_index):
    group_pos = row_index % GROUP
    offsets = [offset for offset in range(1 - GROUP, GROUP) if offset != 0]
    pieces = {}
    for offset in offsets:
        pieces[offset] = from_behind(stacked, "row", offset)
    return pick_members(stacked, pieces, offsets, group_pos)


def fetch_stats(stacked, row_index):
    group_pos = row_index % GROUP
    offsets = [offset for offset in range(1 - GROUP, GROUP) if offset != 0]
    pieces = {}
    for offset in offsets:
        pieces[offset] = from_behind(stacked, "row", offset)
    return pick_members(stacked, pieces, offsets, group_pos)


def gather_strip(stacked):
    return lax.all_gather(stacked, "row", axis=1, tiled=True)


def shards(query_rows, key_rows, value_rows, out_grad, tissue, w_out):
    row_count, width = query_rows.shape
    head_dim = width // H
    scale_multiplier = head_dim ** (-0.5)
    row_devs = lax.axis_size("row")
    col_devs = lax.axis_size("col")
    row_index = lax.axis_index("row")
    col_index = lax.axis_index("col")
    blocks_dev = row_count // BLOCK
    device_pos = row_index * col_devs + col_index
    own_live = jnp.repeat(
        lax.dynamic_slice_in_dim(tissue, device_pos * blocks_dev, blocks_dev, 0), BLOCK
    ).astype(jnp.float32)
    column_flags = jnp.take(tissue.reshape(row_devs, col_devs, blocks_dev), col_index, axis=1)
    group_first = row_index // GROUP * GROUP
    band_blocks = lax.dynamic_slice_in_dim(column_flags, group_first, GROUP, 0).reshape(-1)
    band_flags = jnp.repeat(band_blocks, BLOCK).astype(jnp.float32)
    band_live = jnp.broadcast_to(band_flags[:, None], (GROUP * row_count, H))
    strip_flags = jnp.repeat(column_flags.reshape(-1), BLOCK).astype(jnp.float32)
    strip_live = apply_dilation(jnp.broadcast_to(strip_flags[:, None], (row_devs * row_count, H)))
    own_heads = jnp.broadcast_to(own_live[:, None], (row_count, H))
    query_per_head = query_rows.reshape(row_count, H, head_dim)
    key_per_head = key_rows.reshape(row_count, H, head_dim)
    value_per_head = value_rows.reshape(row_count, H, head_dim)
    band_pair = fetch_rows(jnp.stack([key_rows, value_rows]), row_index)
    band_keys = band_pair[0].reshape(-1, H, head_dim)
    band_values = band_pair[1].reshape(-1, H, head_dim)
    strip_pair = gather_strip(
        jnp.stack(
            [
                apply_dilation(key_per_head).reshape(-1, width),
                apply_dilation(value_per_head).reshape(-1, width),
            ]
        )
    )
    strip_keys = strip_pair[0].reshape(-1, H, head_dim)
    strip_values = strip_pair[1].reshape(-1, H, head_dim)
    attended, logsum_total = forward_rows(
        query_per_head,
        own_live,
        band_keys,
        band_values,
        band_live,
        strip_keys,
        strip_values,
        strip_live,
        scale_multiplier,
    )
    attended_rows = attended.reshape(row_count, width)
    output = jnp.dot(attended_rows, w_out, preferred_element_type=jnp.float32).astype(jnp.bfloat16)
    grad_rows = (
        jnp.dot(out_grad, w_out.T, preferred_element_type=jnp.float32) * own_live[:, None]
    ).astype(jnp.bfloat16)
    gradient_per_head = grad_rows.reshape(row_count, H, head_dim)
    score_gradient = jnp.einsum(
        "qhd,qhd->qh", gradient_per_head, attended, preferred_element_type=jnp.float32
    )
    weight_term = jnp.dot(attended_rows.T, out_grad, preferred_element_type=jnp.float32)
    weight_share = lax.psum_scatter(weight_term, "row", scatter_dimension=1, tiled=True)
    weight_grad = lax.psum(weight_share, "col")
    band_query_pair = fetch_rows(jnp.stack([query_rows, grad_rows]), row_index)
    band_stat_pair = fetch_stats(jnp.stack([logsum_total, score_gradient]), row_index)
    strip_query_pair = gather_strip(
        jnp.stack(
            [
                apply_dilation(query_per_head).reshape(-1, width),
                apply_dilation(gradient_per_head).reshape(-1, width),
            ]
        )
    )
    strip_stat_pair = lax.all_gather(
        jnp.stack([apply_dilation(logsum_total), apply_dilation(score_gradient)]),
        "row",
        axis=1,
        tiled=True,
    )
    query_grad = query_grads(
        query_per_head,
        gradient_per_head,
        logsum_total,
        score_gradient,
        band_keys,
        band_values,
        band_live,
        strip_keys,
        strip_values,
        strip_live,
        scale_multiplier,
    )
    key_grad, value_grad = key_grads(
        key_per_head,
        value_per_head,
        own_heads,
        band_query_pair[0].reshape(-1, H, head_dim),
        band_query_pair[1].reshape(-1, H, head_dim),
        band_stat_pair[0],
        band_stat_pair[1],
        strip_query_pair[0].reshape(-1, H, head_dim),
        strip_query_pair[1].reshape(-1, H, head_dim),
        strip_stat_pair[0],
        strip_stat_pair[1],
        scale_multiplier,
    )
    return (
        output,
        query_grad.reshape(row_count, width),
        key_grad.reshape(row_count, width),
        value_grad.reshape(row_count, width),
        weight_grad,
    )


MESH = pl.DeviceIdType.MESH
F32 = jnp.float32
BF16 = jnp.bfloat16


def dot_nn(a, b):
    return lax.dot_general(a, b, (((1,), (0,)), ((), ())), preferred_element_type=F32)


def dot_nt(a, b):
    return lax.dot_general(a, b, (((1,), (1,)), ((), ())), preferred_element_type=F32)


def dot_tn(a, b):
    return lax.dot_general(a, b, (((0,), (0,)), ((), ())), preferred_element_type=F32)


def column_kernel(
    R, C, HP, HD, N, QC,
    tissue_hbm, q_hbm, k_hbm, v_hbm, og_hbm, w_hbm,
    out_ref, dq_ref, dk_ref, dv_ref, wg_ref,
    tissue_ref, q_ref, k_ref, v_ref, og_ref, w_ref, load_sem,
    tx, rx, otx, orx, gtx, grx, ogt, ctx, crx, ztx, z1rx, z2tx, z2rx, frx,
    bias, probs, dsc, ready, column_in, all_in,
    a_send, a_recv, o_send, o_recv, g_send, g_recv,
    c_send, c_recv, z1_send, z1_recv, z2_send, z2_recv, f_send, f_recv,
):
    T = R * N
    HR = R * HD
    WQ = HP * HD // C
    me = lax.axis_index("row")
    col = lax.axis_index("col")
    core = col % 2
    half, parity = me // 2, me % 2
    scale = HD ** (-0.5)

    def heads(i):
        return slice(i * HR, (i + 1) * HR)

    barrier = pltpu.get_barrier_semaphore()
    for d in range(1, R):
        @pl.when(me + d < R)
        def _():
            pl.semaphore_signal(barrier, inc=1, device_id={"row": me + d}, device_id_type=MESH)

    @pl.when(me == 0)
    def _():
        for d in range(1, C):
            pl.semaphore_signal(
                barrier, inc=1, device_id={"col": (col + d) % C}, device_id_type=MESH
            )

    loads = []

    def load(src, dst):
        copy = pltpu.make_async_copy(src, dst, load_sem.at[len(loads)])
        copy.start()
        loads.append(copy)
        return copy

    qkv_loads = []
    w_loads = []
    for i in range(HP):
        qkv_loads.append([
            load(src.at[:, heads(i)], dst.at[:, heads(i)])
            for src, dst in ((q_hbm, q_ref), (k_hbm, k_ref), (v_hbm, v_ref))
        ])
        if i == 0:
            tissue_load = load(tissue_hbm, tissue_ref)
            og_load = load(og_hbm, og_ref)
        w_loads.append(load(w_hbm.at[heads(i)], w_ref.at[heads(i)]))

    def row_copy(src, dst, send, recv, to):
        return pltpu.make_async_remote_copy(
            src_ref=src, dst_ref=dst, send_sem=send, recv_sem=recv,
            device_id={"row": to}, device_id_type=MESH,
        )

    def col_copy(src, dst, send, recv, to):
        return pltpu.make_async_remote_copy(
            src_ref=src, dst_ref=dst, send_sem=send, recv_sem=recv,
            device_id={"col": to}, device_id_type=MESH,
        )

    pending = []

    def start(copy):
        copy.start()
        pending.append(copy)

    far = (R - 1 - me, (me + 2) % R, me + 1 - 2 * parity)
    others = (C - 1 - col, (col + 2) % C, col + 1 - 2 * core)
    twin, level = far[2], far[1]

    parcels = tuple((i, 0, 3) for i in range(HP)) + tuple((i, 3, 1) for i in range(HP))

    def parcel(n, to):
        i, a, count = parcels[n]
        return row_copy(
            tx.at[to, i, pl.ds(a, count)], rx.at[i, me, pl.ds(a, count)],
            a_send.at[n, to], a_recv.at[n, me], to,
        )

    def send_parcel(n):
        for to in far:
            start(parcel(n, to))

    def send_parcel_of(which, n):
        @pl.when(core == which)
        def _():
            for to in far:
                parcel(n, to).start()

    def sent_parcel(n):
        pending.extend(parcel(n, to) for to in far)

    def wait_parcel(n):
        i, a, count = parcels[n]
        for src in far:
            row_copy(
                tx.at[src, i, pl.ds(a, count)], rx.at[i, src, pl.ds(a, count)],
                a_send.at[n, src], a_recv.at[n, src], src,
            ).wait_recv()

    def pack(i):
        for a, ref in enumerate((q_ref, k_ref, v_ref)):
            qkv_loads[i][a].wait()
            value = ref[:, heads(i)].astype(F32)
            if a == 0:
                value = value * scale
            value = value.T.astype(BF16)
            for d in range(R):
                tx[d, i, a] = value[d * HD : (d + 1) * HD]

    def live_lanes(count, first):
        lane = lax.broadcasted_iota(jnp.int32, (1, count * BLOCK), 1)
        live = jnp.zeros((1, count * BLOCK), F32)
        for j in range(count):
            live = jnp.where(lane // BLOCK == j, tissue_ref[first + j].astype(F32), live)
        return live

    def pack_grads():
        og_load.wait()
        own_live = live_lanes(per_dev, (me * C + col) * per_dev)
        for i in range(HP):
            w_loads[i].wait()
            value = (dot_nt(w_ref[heads(i), :], og_ref[...]) * own_live).astype(BF16)
            for d in range(R):
                tx[d, i, 3] = value[d * HD : (d + 1) * HD]
            rx[i, me, 3] = tx[me, i, 3]

    def turn_grads():
        ogt[...] = og_ref[...].astype(F32).T.astype(BF16)

    def wait_all_in():
        @pl.when(me > 0)
        def _():
            pl.semaphore_wait(all_in, 1)

    per_dev = N // BLOCK
    pl.semaphore_wait(barrier, jnp.where(me == 0, C - 1, me))
    for d in range(1, R):
        @pl.when(me - d >= 0)
        def _():
            pl.semaphore_signal(ready.at[me], inc=1, device_id={"row": me - d}, device_id_type=MESH)

    pack(0)
    for d in range(R - 1):
        to = jnp.where(d < me, d, d + 1)

        @pl.when(to > me)
        def _():
            pl.semaphore_wait(ready.at[to], 1)

        start(parcel(0, to))

    pack(1)
    send_parcel_of(0, 1)

    @pl.when(me == 0)
    def _():
        for d in range(1, C):
            pl.semaphore_signal(
                column_in, inc=1, device_id={"col": (col + d) % C}, device_id_type=MESH
            )
        pl.semaphore_wait(column_in, C - 1)
        for d in range(1, R):
            pl.semaphore_signal(all_in, inc=1, device_id={"row": d}, device_id_type=MESH)

    pack(2)
    for i in range(HP):
        rx[i, me, 0:3] = tx[me, i, 0:3]
    tissue_load.wait()

    krow = lax.broadcasted_iota(jnp.int32, (BLOCK, QC), 0) % DILATION_STEP
    qlane = lax.broadcasted_iota(jnp.int32, (BLOCK, QC), 1) % DILATION_STEP
    twice = jnp.where((krow == me) & (qlane == me), math.log(2.0), 0.0)
    lane = lax.broadcasted_iota(jnp.int32, (1, T), 1)
    qlive = jnp.zeros((1, T), F32)
    for s in range(R):
        for b in range(per_dev):
            flag = tissue_ref[(s * C + col) * per_dev + b].astype(F32)
            j = s * per_dev + b
            bias[j * BLOCK : (j + 1) * BLOCK, :] = twice + (1.0 - flag) * NEG_FILL
            qlive = jnp.where(lane // BLOCK == j, flag, qlive)

    def gathered(i, a):
        return jnp.concatenate([rx[i, s, a] for s in range(R)], axis=1)

    attended = {}

    def forward(i):
        qt, kt, vt = gathered(i, 0), gathered(i, 1), gathered(i, 2)
        parts = []
        for c in range(T // QC):
            cols = slice(c * QC, (c + 1) * QC)
            s = dot_tn(kt, qt[:, cols]) + bias[...]
            top = jnp.max(s, axis=0, keepdims=True)
            p = jnp.exp(s - top)
            total = jnp.sum(p, axis=0, keepdims=True)
            pb = (p * (1.0 / total)).astype(BF16)
            probs[i, :, cols] = pb
            parts.append(dot_nn(vt, pb) * qlive[:, cols])
        o = jnp.concatenate(parts, axis=1).astype(BF16)
        attended[i] = o
        for d in range(R):
            otx[d, i] = o[:, d * N : (d + 1) * N]
        for to in far:
            start(row_copy(otx.at[to, i], orx.at[i, me], o_send.at[i, to], o_recv.at[i, me], to))
        orx[i, me] = otx[me, i]

    def backward(i):
        qt, kt, vt, g = (gathered(i, a) for a in range(4))
        dots = jnp.sum(g.astype(F32) * attended[i].astype(F32), axis=0, keepdims=True)
        parts = []
        for c in range(T // QC):
            cols = slice(c * QC, (c + 1) * QC)
            dp = dot_tn(vt, g[:, cols])
            ds = (probs[i, :, cols].astype(F32) * (dp - dots[:, cols])).astype(BF16)
            dsc[:, cols] = ds
            parts.append(dot_nn(kt, ds) * scale)
        results = (
            jnp.concatenate(parts, axis=1),
            dot_nt(qt, dsc[...]),
            dot_nt(g, probs[i]),
        )
        for a, value in enumerate(results):
            value = value.astype(BF16)
            for d in range(R):
                gtx[d, i, a] = value[:, d * N : (d + 1) * N]
        grx[i, me] = gtx[me, i]

    def grads_copy(i, a, count, src, dst, to):
        return row_copy(
            gtx.at[src, i, pl.ds(a, count)], grx.at[i, dst, pl.ds(a, count)],
            g_send.at[i, a, src], g_recv.at[i, a, dst], to,
        )

    splits = ((0, 3),), ((0, 1), (1, 2)), ((0, 1), (1, 2))

    def send_grads(i, part=0):
        a, count = splits[i][part]
        for to in far:
            start(grads_copy(i, a, count, to, me, to))

    def send_grads_of(which, i, part=0):
        a, count = splits[i][part]

        @pl.when(core == which)
        def _():
            for to in far:
                grads_copy(i, a, count, to, me, to).start()

    def sent_grads(i):
        for a, count in splits[i]:
            pending.extend(grads_copy(i, a, count, to, me, to) for to in far)

    def wait_o(i):
        for src in far:
            row_copy(
                otx.at[src, i], orx.at[i, src], o_send.at[i, src], o_recv.at[i, src], src
            ).wait_recv()

    def weight_core(i):
        wait_o(i)
        term = dot_nt(ogt[...], orx[i].reshape(HR, N)).astype(BF16)
        for r in range(R):
            for c in range(C):
                first = (r * C + c) * WQ
                ctx[i, c, r] = term[first : first + WQ]
        for to in others:
            start(col_copy(ctx.at[i, to], crx.at[i, col], c_send.at[i, to], c_recv.at[i, col], to))

    def wait_c(i):
        for src in others:
            col_copy(
                ctx.at[i, src], crx.at[i, src], c_send.at[i, src], c_recv.at[i, src], src
            ).wait_recv()

    def weight_twin(i):
        wait_c(i)
        share = ctx[i, col].astype(F32)
        for src in others:
            share = share + crx[i, src].astype(F32)
        share = share.astype(BF16)
        for r in range(R):
            ztx[i, r % 2, r // 2] = share[r]
        start(row_copy(ztx.at[i, 1 - parity], z1rx.at[i], z1_send.at[i], z1_recv.at[i], twin))

    def wait_z1(i):
        row_copy(ztx.at[i, 1 - parity], z1rx.at[i], z1_send.at[i], z1_recv.at[i], twin).wait_recv()

    def weight_level(i):
        wait_z1(i)
        z2tx[i] = (ztx[i, parity].astype(F32) + z1rx[i].astype(F32)).astype(BF16)
        start(row_copy(z2tx.at[i, 1 - half], z2rx.at[i], z2_send.at[i], z2_recv.at[i], level))

    def wait_z2(i):
        row_copy(z2tx.at[i, 1 - half], z2rx.at[i], z2_send.at[i], z2_recv.at[i], level).wait_recv()

    def weight_spread(i):
        wait_z2(i)
        frx[i, col] = (z2tx[i, half].astype(F32) + z2rx[i].astype(F32)).astype(BF16)
        for to in others:
            start(col_copy(frx.at[i, col], frx.at[i, col], f_send.at[i, to], f_recv.at[i, col], to))

    def wait_f(i):
        for src in others:
            col_copy(
                frx.at[i, src], frx.at[i, src], f_send.at[i, src], f_recv.at[i, src], src
            ).wait_recv()

    def weight_write(i):
        wait_f(i)
        wg_ref[:, heads(i)] = frx[i].reshape(C * WQ, HR).astype(F32)

    def wait_g(i):
        for a, count in splits[i]:
            for src in far:
                grads_copy(i, a, count, src, src, src).wait_recv()

    def grads_write(i):
        wait_g(i)
        for a, ref in enumerate((dq_ref, dk_ref, dv_ref)):
            value = jnp.concatenate([grx[i, s, a] for s in range(R)], axis=0)
            ref[:, heads(i)] = value.astype(F32).T.astype(BF16)

    pack_grads()
    turn_grads()
    wait_parcel(0)
    forward(0)
    send_parcel_of(1, 1)
    send_parcel_of(0, 2)
    wait_parcel(1)
    forward(1)
    send_parcel_of(1, 2)
    send_parcel(3)
    wait_all_in()
    weight_core(0)
    wait_parcel(2)
    forward(2)
    send_parcel(4)
    weight_core(1)
    send_parcel(5)
    wait_parcel(3)
    backward(0)
    send_grads_of(0, 0)
    send_grads_of(1, 0)
    weight_core(2)
    weight_twin(0)
    wait_parcel(4)
    backward(1)
    send_grads_of(0, 1, 0)
    send_grads_of(1, 1, 0)
    weight_twin(1)
    weight_level(0)
    wait_parcel(5)
    backward(2)
    weight_twin(2)
    send_grads_of(0, 1, 1)
    send_grads_of(1, 1, 1)
    weight_level(1)
    weight_level(2)
    send_grads_of(0, 2, 0)
    send_grads_of(1, 2, 0)
    send_grads_of(0, 2, 1)
    send_grads_of(1, 2, 1)
    sent_parcel(1)
    sent_parcel(2)
    sent_grads(0)
    sent_grads(1)
    sent_grads(2)
    out_ref[...] = dot_tn(orx[...].reshape(HP * HR, N), w_ref[...]).astype(BF16)
    weight_spread(0)
    weight_spread(1)
    grads_write(0)
    weight_write(0)
    weight_spread(2)
    grads_write(1)
    weight_write(1)
    weight_write(2)
    grads_write(2)

    for copy in pending:
        copy.wait_send()


def write_kernel(*refs):
    held, outs, store_sem = refs[:5], refs[5:10], refs[10]
    stores = [pltpu.make_async_copy(held[n], outs[n], store_sem.at[n]) for n in range(5)]
    for store in stores:
        store.start()
    for store in stores:
        store.wait()


def column_shards(query_rows, key_rows, value_rows, out_grad, tissue, w_out):
    N, width = query_rows.shape
    R = lax.axis_size("row")
    C = lax.axis_size("col")
    HP = H // R
    HD = width // H
    HR = R * HD
    HW = HP * HD
    T = R * N
    WQ = HW // C
    QC = 256
    vmem = pl.BlockSpec(memory_space=pltpu.VMEM)
    hbm = pl.BlockSpec(memory_space=pltpu.HBM)
    dma = pltpu.SemaphoreType.DMA
    rows = jax.ShapeDtypeStruct((N, width), BF16)
    shapes = (rows, rows, rows, rows, jax.ShapeDtypeStruct((HW, width), F32))
    operands = (tissue, query_rows, key_rows, value_rows, out_grad, w_out)
    results = pl.pallas_call(
        functools.partial(column_kernel, R, C, HP, HD, N, QC),
        out_shape=tuple(pltpu.VMEM(s.shape, s.dtype) for s in shapes),
        in_specs=[hbm] * 6,
        out_specs=(vmem,) * 5,
        scratch_shapes=[
            pltpu.SMEM(tissue.shape, jnp.int32),
            pltpu.VMEM((N, width), BF16),
            pltpu.VMEM((N, width), BF16),
            pltpu.VMEM((N, width), BF16),
            pltpu.VMEM((N, width), BF16),
            pltpu.VMEM((width, width), BF16),
            dma((4 * HP + 2,)),
            pltpu.VMEM((R, HP, 4, HD, N), BF16),
            pltpu.VMEM((HP, R, 4, HD, N), BF16),
            pltpu.VMEM((R, HP, HD, N), BF16),
            pltpu.VMEM((HP, R, HD, N), BF16),
            pltpu.VMEM((R, HP, 3, HD, N), BF16),
            pltpu.VMEM((HP, R, 3, HD, N), BF16),
            pltpu.VMEM((width, N), BF16),
            pltpu.VMEM((HP, C, R, WQ, HR), BF16),
            pltpu.VMEM((HP, C, R, WQ, HR), BF16),
            pltpu.VMEM((HP, 2, 2, WQ, HR), BF16),
            pltpu.VMEM((HP, 2, WQ, HR), BF16),
            pltpu.VMEM((HP, 2, WQ, HR), BF16),
            pltpu.VMEM((HP, WQ, HR), BF16),
            pltpu.VMEM((HP, C, WQ, HR), BF16),
            pltpu.VMEM((T, QC), F32),
            pltpu.VMEM((HP, T, T), BF16),
            pltpu.VMEM((T, T), BF16),
            pltpu.SemaphoreType.REGULAR((R,)),
            pltpu.SemaphoreType.REGULAR,
            pltpu.SemaphoreType.REGULAR,
            dma((2 * HP, R)), dma((2 * HP, R)),
            dma((HP, R)), dma((HP, R)),
            dma((HP, 3, R)), dma((HP, 3, R)),
            dma((HP, C)), dma((HP, C)),
            dma((HP,)), dma((HP,)),
            dma((HP,)), dma((HP,)),
            dma((HP, C)), dma((HP, C)),
        ],
        compiler_params=pltpu.CompilerParams(
            collective_id=0, has_side_effects=True, vmem_limit_bytes=40 * 2**20
        ),
    )(*(pltpu.with_memory_space_constraint(x, pltpu.HBM) for x in operands))
    *four, weight_t = pl.pallas_call(
        write_kernel,
        out_shape=shapes,
        in_specs=[vmem] * 5,
        out_specs=(hbm,) * 5,
        scratch_shapes=[dma((5,))],
        compiler_params=pltpu.CompilerParams(vmem_limit_bytes=2**20),
    )(*(pltpu.with_memory_space_constraint(x, pltpu.VMEM) for x in results))
    return (*four, weight_t.T)


def solution(mesh):
    in_specs = (
        P(("slides", "row", "col"), None),
        P(("slides", "row", "col"), None),
        P(("slides", "row", "col"), None),
        P(("slides", "row", "col"), None),
        P("slides"),
        P(),
    )
    out_specs = (
        P(("slides", "row", "col"), None),
        P(("slides", "row", "col"), None),
        P(("slides", "row", "col"), None),
        P(("slides", "row", "col"), None),
        P("slides", "row"),
    )
    whole_column = mesh.shape["row"] == GROUP and mesh.shape["col"] == 4
    body = column_shards if whole_column else shards
    return jax.shard_map(body, mesh=mesh, in_specs=in_specs, out_specs=out_specs, check_vma=False)
```

```python
import functools
import math

import jax
import jax.numpy as jnp
from jax import lax
from jax.experimental import pallas as pl
from jax.experimental.pallas import tpu as pltpu
from jax.sharding import PartitionSpec as P

H = 12
DILATION_STEP = 4
GROUP = 4
BLOCK = 64


NEG_FILL = -1e30


def from_behind(array, axis, by):
    devices = lax.axis_size(axis)
    pairs = [(i, i + by) for i in range(devices) if 0 <= i + by < devices]
    return lax.ppermute(array, axis, pairs)


def apply_dilation(input_array):
    head_number = input_array.shape[1]
    divide_rows = input_array.reshape(
        (input_array.shape[0] // DILATION_STEP, DILATION_STEP) + input_array.shape[1:]
    )
    return jnp.stack(
        [
            divide_rows[:, head_index % DILATION_STEP, head_index]
            for head_index in range(head_number)
        ],
        axis=1,
    )


def undilate(input_array, fill_value):
    head_number = input_array.shape[1]
    selected_rows = (
        jnp.arange(DILATION_STEP)[:, None] == (jnp.arange(head_number) % DILATION_STEP)[None, :]
    )
    selected_rows = selected_rows.reshape(
        (1, DILATION_STEP, head_number) + (1,) * (input_array.ndim - 2)
    )
    scatter_back = jnp.where(
        selected_rows, input_array[:, None], jnp.asarray(fill_value, input_array.dtype)
    )
    return scatter_back.reshape((input_array.shape[0] * DILATION_STEP,) + input_array.shape[1:])


def product(form, left, right):
    return jnp.einsum(form, left, right, preferred_element_type=jnp.float32)


def masked_scores(queries, keys_in, key_live, scale_multiplier):
    raw_scores = product("qhd,khd->hqk", queries, keys_in) * scale_multiplier
    return jnp.where(key_live.T[:, None, :] > 0, raw_scores, NEG_FILL)


def forward_rows(
    queries,
    query_live,
    band_keys,
    band_values,
    band_live,
    strip_keys,
    strip_values,
    strip_live,
    scale_multiplier,
):
    scores_band = masked_scores(queries, band_keys, band_live, scale_multiplier)
    scores_strip = masked_scores(apply_dilation(queries), strip_keys, strip_live, scale_multiplier)
    top_rows = jnp.maximum(scores_band.max(-1).T, undilate(scores_strip.max(-1).T, NEG_FILL))
    total_band = jnp.sum(jnp.exp(scores_band - top_rows.T[:, :, None]), -1).T
    total_strip = jnp.sum(jnp.exp(scores_strip - apply_dilation(top_rows).T[:, :, None]), -1).T
    logsum_total = top_rows + jnp.log(total_band + undilate(total_strip, 0.0))
    weights_band = jnp.exp(scores_band - logsum_total.T[:, :, None]).astype(jnp.bfloat16)
    weights_strip = jnp.exp(scores_strip - apply_dilation(logsum_total).T[:, :, None]).astype(
        jnp.bfloat16
    )
    combined = product("hqk,khd->qhd", weights_band, band_values)
    combined = combined + undilate(product("hqk,khd->qhd", weights_strip, strip_values), 0.0)
    return ((combined * query_live[:, None, None]).astype(jnp.bfloat16), logsum_total)


def query_branch(
    queries, grads, lse_rows, dot_rows, keys_in, values_in, key_live, scale_multiplier
):
    scores = masked_scores(queries, keys_in, key_live, scale_multiplier)
    probs = jnp.exp(scores - lse_rows.T[:, :, None])
    dprobs = product("qhd,khd->hqk", grads, values_in)
    dscores = (probs * (dprobs - dot_rows.T[:, :, None])).astype(jnp.bfloat16)
    return product("hqk,khd->qhd", dscores, keys_in)


def query_grads(
    queries,
    grads,
    lse_rows,
    dot_rows,
    band_keys,
    band_values,
    band_live,
    strip_keys,
    strip_values,
    strip_live,
    scale_multiplier,
):
    first_part = query_branch(
        queries, grads, lse_rows, dot_rows, band_keys, band_values, band_live, scale_multiplier
    )
    second_part = query_branch(
        apply_dilation(queries),
        apply_dilation(grads),
        apply_dilation(lse_rows),
        apply_dilation(dot_rows),
        strip_keys,
        strip_values,
        strip_live,
        scale_multiplier,
    )
    return ((first_part + undilate(second_part, 0.0)) * scale_multiplier).astype(jnp.bfloat16)


def key_branch(keys_in, values_in, key_live, queries, grads, lse_rows, dot_rows, scale_multiplier):
    scores = masked_scores(queries, keys_in, key_live, scale_multiplier)
    probs = jnp.exp(scores - lse_rows.T[:, :, None])
    dprobs = product("qhd,khd->hqk", grads, values_in)
    dscores = (probs * (dprobs - dot_rows.T[:, :, None])).astype(jnp.bfloat16)
    key_part = product("hqk,qhd->khd", dscores, queries)
    value_part = product("hqk,qhd->khd", probs.astype(jnp.bfloat16), grads)
    return (key_part, value_part)


def key_grads(
    keys_in,
    values_in,
    key_live,
    band_queries,
    band_grads,
    band_lse,
    band_dot,
    strip_queries,
    strip_grads,
    strip_lse,
    strip_dot,
    scale_multiplier,
):
    key_one, value_one = key_branch(
        keys_in, values_in, key_live, band_queries, band_grads, band_lse, band_dot, scale_multiplier
    )
    key_two, value_two = key_branch(
        apply_dilation(keys_in),
        apply_dilation(values_in),
        apply_dilation(key_live),
        strip_queries,
        strip_grads,
        strip_lse,
        strip_dot,
        scale_multiplier,
    )
    key_total = ((key_one + undilate(key_two, 0.0)) * scale_multiplier).astype(jnp.bfloat16)
    value_total = (value_one + undilate(value_two, 0.0)).astype(jnp.bfloat16)
    return (key_total, value_total)


def pick_members(stacked, pieces, offsets, group_pos):
    members = []
    for member in range(GROUP):
        piece = stacked
        for offset in offsets:
            piece = jnp.where(group_pos - member == offset, pieces[offset], piece)
        members.append(piece)
    return jnp.concatenate(members, 1)


def fetch_rows(stacked, row_index):
    group_pos = row_index % GROUP
    offsets = [offset for offset in range(1 - GROUP, GROUP) if offset != 0]
    pieces = {}
    for offset in offsets:
        pieces[offset] = from_behind(stacked, "row", offset)
    return pick_members(stacked, pieces, offsets, group_pos)


def fetch_stats(stacked, row_index):
    group_pos = row_index % GROUP
    offsets = [offset for offset in range(1 - GROUP, GROUP) if offset != 0]
    pieces = {}
    for offset in offsets:
        pieces[offset] = from_behind(stacked, "row", offset)
    return pick_members(stacked, pieces, offsets, group_pos)


def gather_strip(stacked):
    return lax.all_gather(stacked, "row", axis=1, tiled=True)


def shards(query_rows, key_rows, value_rows, out_grad, tissue, w_out):
    row_count, width = query_rows.shape
    head_dim = width // H
    scale_multiplier = head_dim ** (-0.5)
    row_devs = lax.axis_size("row")
    col_devs = lax.axis_size("col")
    row_index = lax.axis_index("row")
    col_index = lax.axis_index("col")
    blocks_dev = row_count // BLOCK
    device_pos = row_index * col_devs + col_index
    own_live = jnp.repeat(
        lax.dynamic_slice_in_dim(tissue, device_pos * blocks_dev, blocks_dev, 0), BLOCK
    ).astype(jnp.float32)
    column_flags = jnp.take(tissue.reshape(row_devs, col_devs, blocks_dev), col_index, axis=1)
    group_first = row_index // GROUP * GROUP
    band_blocks = lax.dynamic_slice_in_dim(column_flags, group_first, GROUP, 0).reshape(-1)
    band_flags = jnp.repeat(band_blocks, BLOCK).astype(jnp.float32)
    band_live = jnp.broadcast_to(band_flags[:, None], (GROUP * row_count, H))
    strip_flags = jnp.repeat(column_flags.reshape(-1), BLOCK).astype(jnp.float32)
    strip_live = apply_dilation(jnp.broadcast_to(strip_flags[:, None], (row_devs * row_count, H)))
    own_heads = jnp.broadcast_to(own_live[:, None], (row_count, H))
    query_per_head = query_rows.reshape(row_count, H, head_dim)
    key_per_head = key_rows.reshape(row_count, H, head_dim)
    value_per_head = value_rows.reshape(row_count, H, head_dim)
    band_pair = fetch_rows(jnp.stack([key_rows, value_rows]), row_index)
    band_keys = band_pair[0].reshape(-1, H, head_dim)
    band_values = band_pair[1].reshape(-1, H, head_dim)
    strip_pair = gather_strip(
        jnp.stack(
            [
                apply_dilation(key_per_head).reshape(-1, width),
                apply_dilation(value_per_head).reshape(-1, width),
            ]
        )
    )
    strip_keys = strip_pair[0].reshape(-1, H, head_dim)
    strip_values = strip_pair[1].reshape(-1, H, head_dim)
    attended, logsum_total = forward_rows(
        query_per_head,
        own_live,
        band_keys,
        band_values,
        band_live,
        strip_keys,
        strip_values,
        strip_live,
        scale_multiplier,
    )
    attended_rows = attended.reshape(row_count, width)
    output = jnp.dot(attended_rows, w_out, preferred_element_type=jnp.float32).astype(jnp.bfloat16)
    grad_rows = (
        jnp.dot(out_grad, w_out.T, preferred_element_type=jnp.float32) * own_live[:, None]
    ).astype(jnp.bfloat16)
    gradient_per_head = grad_rows.reshape(row_count, H, head_dim)
    score_gradient = jnp.einsum(
        "qhd,qhd->qh", gradient_per_head, attended, preferred_element_type=jnp.float32
    )
    weight_term = jnp.dot(attended_rows.T, out_grad, preferred_element_type=jnp.float32)
    weight_share = lax.psum_scatter(weight_term, "row", scatter_dimension=1, tiled=True)
    weight_grad = lax.psum(weight_share, "col")
    band_query_pair = fetch_rows(jnp.stack([query_rows, grad_rows]), row_index)
    band_stat_pair = fetch_stats(jnp.stack([logsum_total, score_gradient]), row_index)
    strip_query_pair = gather_strip(
        jnp.stack(
            [
                apply_dilation(query_per_head).reshape(-1, width),
                apply_dilation(gradient_per_head).reshape(-1, width),
            ]
        )
    )
    strip_stat_pair = lax.all_gather(
        jnp.stack([apply_dilation(logsum_total), apply_dilation(score_gradient)]),
        "row",
        axis=1,
        tiled=True,
    )
    query_grad = query_grads(
        query_per_head,
        gradient_per_head,
        logsum_total,
        score_gradient,
        band_keys,
        band_values,
        band_live,
        strip_keys,
        strip_values,
        strip_live,
        scale_multiplier,
    )
    key_grad, value_grad = key_grads(
        key_per_head,
        value_per_head,
        own_heads,
        band_query_pair[0].reshape(-1, H, head_dim),
        band_query_pair[1].reshape(-1, H, head_dim),
        band_stat_pair[0],
        band_stat_pair[1],
        strip_query_pair[0].reshape(-1, H, head_dim),
        strip_query_pair[1].reshape(-1, H, head_dim),
        strip_stat_pair[0],
        strip_stat_pair[1],
        scale_multiplier,
    )
    return (
        output,
        query_grad.reshape(row_count, width),
        key_grad.reshape(row_count, width),
        value_grad.reshape(row_count, width),
        weight_grad,
    )


MESH = pl.DeviceIdType.MESH
F32 = jnp.float32
BF16 = jnp.bfloat16


def dot_nn(a, b):
    return lax.dot_general(a, b, (((1,), (0,)), ((), ())), preferred_element_type=F32)


def dot_nt(a, b):
    return lax.dot_general(a, b, (((1,), (1,)), ((), ())), preferred_element_type=F32)


def dot_tn(a, b):
    return lax.dot_general(a, b, (((0,), (0,)), ((), ())), preferred_element_type=F32)


def column_kernel(
    R, C, HP, HD, N, QC,
    tissue_hbm, q_hbm, k_hbm, v_hbm, og_hbm, w_hbm,
    out_ref, dq_ref, dk_ref, dv_ref, wg_ref,
    tissue_ref, q_ref, k_ref, v_ref, og_ref, w_ref, load_sem,
    tx, rx, otx, orx, gtx, grx, ogt, ctx, crx, ztx, z1rx, z2tx, z2rx, frx,
    bias, probs, dsc, ready, column_in, all_in,
    a_send, a_recv, o_send, o_recv, g_send, g_recv,
    c_send, c_recv, z1_send, z1_recv, z2_send, z2_recv, f_send, f_recv,
):
    T = R * N
    HR = R * HD
    WQ = HP * HD // C
    me = lax.axis_index("row")
    col = lax.axis_index("col")
    core = col % 2
    half, parity = me // 2, me % 2
    scale = HD ** (-0.5)

    def heads(i):
        return slice(i * HR, (i + 1) * HR)

    loads = []

    def load(src, dst):
        copy = pltpu.make_async_copy(src, dst, load_sem.at[len(loads)])
        copy.start()
        loads.append(copy)
        return copy

    def load_heads(i):
        return [
            load(src.at[:, heads(i)], dst.at[:, heads(i)])
            for src, dst in ((q_hbm, q_ref), (k_hbm, k_ref), (v_hbm, v_ref))
        ]

    qkv_loads = [load_heads(0)]

    barrier = pltpu.get_barrier_semaphore()
    for d in range(1, R):
        @pl.when(me + d < R)
        def _():
            pl.semaphore_signal(barrier, inc=1, device_id={"row": me + d}, device_id_type=MESH)

    @pl.when(me == 0)
    def _():
        for d in range(1, C):
            pl.semaphore_signal(
                barrier, inc=1, device_id={"col": (col + d) % C}, device_id_type=MESH
            )

    def row_copy(src, dst, send, recv, to):
        return pltpu.make_async_remote_copy(
            src_ref=src, dst_ref=dst, send_sem=send, recv_sem=recv,
            device_id={"row": to}, device_id_type=MESH,
        )

    def col_copy(src, dst, send, recv, to):
        return pltpu.make_async_remote_copy(
            src_ref=src, dst_ref=dst, send_sem=send, recv_sem=recv,
            device_id={"col": to}, device_id_type=MESH,
        )

    pending = []

    def start(copy):
        copy.start()
        pending.append(copy)

    far = (R - 1 - me, (me + 2) % R, me + 1 - 2 * parity)
    others = (C - 1 - col, (col + 2) % C, col + 1 - 2 * core)
    twin, level = far[2], far[1]

    parcels = tuple((i, 0, 3) for i in range(HP)) + tuple((i, 3, 1) for i in range(HP))

    def parcel(n, to):
        i, a, count = parcels[n]
        return row_copy(
            tx.at[to, i, pl.ds(a, count)], rx.at[i, me, pl.ds(a, count)],
            a_send.at[n, to], a_recv.at[n, me], to,
        )

    def send_parcel(n):
        for to in far:
            start(parcel(n, to))

    def send_parcel_of(which, n):
        @pl.when(core == which)
        def _():
            for to in far:
                parcel(n, to).start()

    def sent_parcel(n):
        pending.extend(parcel(n, to) for to in far)

    def wait_parcel(n):
        i, a, count = parcels[n]
        for src in far:
            row_copy(
                tx.at[src, i, pl.ds(a, count)], rx.at[i, src, pl.ds(a, count)],
                a_send.at[n, src], a_recv.at[n, src], src,
            ).wait_recv()

    def pack_one(i, a):
        qkv_loads[i][a].wait()
        value = (q_ref, k_ref, v_ref)[a][:, heads(i)].astype(F32)
        if a == 0:
            value = value * scale
        value = value.T.astype(BF16)
        for d in range(R):
            tx[d, i, a] = value[d * HD : (d + 1) * HD]

    def pack(i):
        for a in range(3):
            pack_one(i, a)

    def live_lanes(count, first):
        lane = lax.broadcasted_iota(jnp.int32, (1, count * BLOCK), 1)
        live = jnp.zeros((1, count * BLOCK), F32)
        for j in range(count):
            live = jnp.where(lane // BLOCK == j, tissue_ref[first + j].astype(F32), live)
        return live

    def pack_grads():
        og_load.wait()
        own_live = live_lanes(per_dev, (me * C + col) * per_dev)
        for i in range(HP):
            w_loads[i].wait()
            value = (dot_nt(w_ref[heads(i), :], og_ref[...]) * own_live).astype(BF16)
            for d in range(R):
                tx[d, i, 3] = value[d * HD : (d + 1) * HD]
            rx[i, me, 3] = tx[me, i, 3]

    def turn_grads():
        ogt[...] = og_ref[...].astype(F32).T.astype(BF16)

    def wait_all_in():
        @pl.when(me > 0)
        def _():
            pl.semaphore_wait(all_in, 1)

    per_dev = N // BLOCK
    pl.semaphore_wait(barrier, jnp.where(me == 0, C - 1, me))
    for d in range(1, R):
        @pl.when(me - d >= 0)
        def _():
            pl.semaphore_signal(ready.at[me], inc=1, device_id={"row": me - d}, device_id_type=MESH)

    for a in range(3):
        pack_one(0, a)
        for d in range(R - 1, 0, -1):
            @pl.when(me - d >= 0)
            def _():
                row_copy(
                    tx.at[me - d, 0, pl.ds(a, 1)], rx.at[0, me, pl.ds(a, 1)],
                    a_send.at[0, me - d], a_recv.at[0, me], me - d,
                ).start()

    qkv_loads.append(load_heads(1))
    tissue_load = load(tissue_hbm, tissue_ref)
    og_load = load(og_hbm, og_ref)
    w_loads = [load(w_hbm.at[heads(i)], w_ref.at[heads(i)]) for i in range(HP)]
    qkv_loads.append(load_heads(2))
    for d in range(1, R):
        @pl.when(me + d < R)
        def _():
            pl.semaphore_wait(ready.at[me + d], 1)
            parcel(0, me + d).start()

    pending.extend(parcel(0, to) for to in far)
    pack(1)
    send_parcel_of(0, 1)

    @pl.when(me == 0)
    def _():
        for d in range(1, C):
            pl.semaphore_signal(
                column_in, inc=1, device_id={"col": (col + d) % C}, device_id_type=MESH
            )
        pl.semaphore_wait(column_in, C - 1)
        for d in range(1, R):
            pl.semaphore_signal(all_in, inc=1, device_id={"row": d}, device_id_type=MESH)

    pack(2)
    for i in range(HP):
        rx[i, me, 0:3] = tx[me, i, 0:3]
    tissue_load.wait()

    krow = lax.broadcasted_iota(jnp.int32, (BLOCK, QC), 0) % DILATION_STEP
    qlane = lax.broadcasted_iota(jnp.int32, (BLOCK, QC), 1) % DILATION_STEP
    twice = jnp.where((krow == me) & (qlane == me), math.log(2.0), 0.0)
    lane = lax.broadcasted_iota(jnp.int32, (1, T), 1)
    qlive = jnp.zeros((1, T), F32)
    for s in range(R):
        for b in range(per_dev):
            flag = tissue_ref[(s * C + col) * per_dev + b].astype(F32)
            j = s * per_dev + b
            bias[j * BLOCK : (j + 1) * BLOCK, :] = twice + (1.0 - flag) * NEG_FILL
            qlive = jnp.where(lane // BLOCK == j, flag, qlive)

    def gathered(i, a):
        return jnp.concatenate([rx[i, s, a] for s in range(R)], axis=1)

    attended = {}

    def forward(i):
        qt, kt, vt = gathered(i, 0), gathered(i, 1), gathered(i, 2)
        parts = []
        for c in range(T // QC):
            cols = slice(c * QC, (c + 1) * QC)
            s = dot_tn(kt, qt[:, cols]) + bias[...]
            top = jnp.max(s, axis=0, keepdims=True)
            p = jnp.exp(s - top)
            total = jnp.sum(p, axis=0, keepdims=True)
            pb = (p * (1.0 / total)).astype(BF16)
            probs[i, :, cols] = pb
            parts.append(dot_nn(vt, pb) * qlive[:, cols])
        o = jnp.concatenate(parts, axis=1).astype(BF16)
        attended[i] = o
        for d in range(R):
            otx[d, i] = o[:, d * N : (d + 1) * N]
        for to in far:
            start(row_copy(otx.at[to, i], orx.at[i, me], o_send.at[i, to], o_recv.at[i, me], to))
        orx[i, me] = otx[me, i]

    def backward(i):
        qt, kt, vt, g = (gathered(i, a) for a in range(4))
        dots = jnp.sum(g.astype(F32) * attended[i].astype(F32), axis=0, keepdims=True)
        parts = []
        for c in range(T // QC):
            cols = slice(c * QC, (c + 1) * QC)
            dp = dot_tn(vt, g[:, cols])
            ds = (probs[i, :, cols].astype(F32) * (dp - dots[:, cols])).astype(BF16)
            dsc[:, cols] = ds
            parts.append(dot_nn(kt, ds) * scale)
        results = (
            jnp.concatenate(parts, axis=1),
            dot_nt(qt, dsc[...]),
            dot_nt(g, probs[i]),
        )
        for a, value in enumerate(results):
            value = value.astype(BF16)
            for d in range(R):
                gtx[d, i, a] = value[:, d * N : (d + 1) * N]
        grx[i, me] = gtx[me, i]

    def grads_copy(i, a, count, src, dst, to):
        return row_copy(
            gtx.at[src, i, pl.ds(a, count)], grx.at[i, dst, pl.ds(a, count)],
            g_send.at[i, a, src], g_recv.at[i, a, dst], to,
        )

    splits = ((0, 3),), ((0, 1), (1, 2)), ((0, 2), (2, 1))

    def send_grads(i, part=0):
        a, count = splits[i][part]
        for to in far:
            start(grads_copy(i, a, count, to, me, to))

    def send_grads_of(which, i, part=0):
        a, count = splits[i][part]

        order = far if i < HP - 1 else [jnp.where(d < me, d, d + 1) for d in range(R - 1)]

        @pl.when(core == which)
        def _():
            for to in order:
                grads_copy(i, a, count, to, me, to).start()

    def sent_grads(i):
        for a, count in splits[i]:
            pending.extend(grads_copy(i, a, count, to, me, to) for to in far)

    def wait_o(i):
        for src in far:
            row_copy(
                otx.at[src, i], orx.at[i, src], o_send.at[i, src], o_recv.at[i, src], src
            ).wait_recv()

    def weight_core(i):
        wait_o(i)
        term = dot_nt(ogt[...], orx[i].reshape(HR, N)).astype(BF16)
        for r in range(R):
            for c in range(C):
                first = (r * C + c) * WQ
                ctx[i, c, r] = term[first : first + WQ]
        for to in others:
            start(col_copy(ctx.at[i, to], crx.at[i, col], c_send.at[i, to], c_recv.at[i, col], to))

    def wait_c(i):
        for src in others:
            col_copy(
                ctx.at[i, src], crx.at[i, src], c_send.at[i, src], c_recv.at[i, src], src
            ).wait_recv()

    def weight_twin(i):
        wait_c(i)
        share = ctx[i, col].astype(F32)
        for src in others:
            share = share + crx[i, src].astype(F32)
        share = share.astype(BF16)
        for r in range(R):
            ztx[i, r % 2, r // 2] = share[r]
        start(row_copy(ztx.at[i, 1 - parity], z1rx.at[i], z1_send.at[i], z1_recv.at[i], twin))

    def wait_z1(i):
        row_copy(ztx.at[i, 1 - parity], z1rx.at[i], z1_send.at[i], z1_recv.at[i], twin).wait_recv()

    def weight_level(i):
        wait_z1(i)
        z2tx[i] = (ztx[i, parity].astype(F32) + z1rx[i].astype(F32)).astype(BF16)
        start(row_copy(z2tx.at[i, 1 - half], z2rx.at[i], z2_send.at[i], z2_recv.at[i], level))

    def wait_z2(i):
        row_copy(z2tx.at[i, 1 - half], z2rx.at[i], z2_send.at[i], z2_recv.at[i], level).wait_recv()

    def weight_spread(i):
        wait_z2(i)
        frx[i, col] = (z2tx[i, half].astype(F32) + z2rx[i].astype(F32)).astype(BF16)
        for to in others:
            start(col_copy(frx.at[i, col], frx.at[i, col], f_send.at[i, to], f_recv.at[i, col], to))

    def wait_f(i):
        for src in others:
            col_copy(
                frx.at[i, src], frx.at[i, src], f_send.at[i, src], f_recv.at[i, src], src
            ).wait_recv()

    def weight_write(i):
        wait_f(i)
        wg_ref[:, heads(i)] = frx[i].reshape(C * WQ, HR).astype(F32)

    def wait_part(i, a, count):
        for src in far:
            grads_copy(i, a, count, src, src, src).wait_recv()

    def wait_g(i):
        for a, count in splits[i]:
            wait_part(i, a, count)

    def grads_write(i):
        refs = (dq_ref, dk_ref, dv_ref)
        for first, count in splits[i]:
            wait_part(i, first, count)
            for a in range(first, first + count):
                value = grx[i, :, a].reshape(HR, N)
                refs[a][:, heads(i)] = value.astype(F32).T.astype(BF16)

    def drain():
        for copy in pending:
            copy.wait_send()
        pending.clear()

    pack_grads()
    turn_grads()
    wait_parcel(0)
    forward(0)
    send_parcel_of(1, 1)
    wait_all_in()
    sent_parcel(1)
    send_parcel_of(0, 2)
    wait_parcel(1)
    forward(1)
    send_parcel_of(1, 2)
    send_parcel(3)
    weight_core(0)
    wait_parcel(2)
    forward(2)
    send_parcel(4)
    weight_core(1)
    send_parcel(5)
    wait_parcel(3)
    backward(0)
    send_grads_of(0, 0, 0)
    send_grads_of(1, 0, 0)
    weight_core(2)
    weight_twin(0)
    wait_parcel(4)
    backward(1)
    weight_level(0)
    send_grads_of(0, 1, 0)
    send_grads_of(1, 1, 0)
    send_grads_of(0, 1, 1)
    weight_twin(1)
    wait_parcel(5)
    backward(2)
    weight_twin(2)
    send_grads_of(1, 1, 1)
    weight_level(1)
    weight_level(2)
    send_grads_of(0, 2, 0)
    send_grads_of(1, 2, 0)
    send_grads_of(0, 2, 1)
    send_grads_of(1, 2, 1)
    sent_parcel(2)
    sent_grads(0)
    sent_grads(1)
    weight_spread(0)
    out_ref[...] = dot_tn(orx[...].reshape(HP * HR, N), w_ref[...]).astype(BF16)
    weight_spread(1)
    weight_spread(2)
    grads_write(0)
    grads_write(1)
    weight_write(0)
    weight_write(1)
    weight_write(2)
    drain()
    sent_grads(2)
    grads_write(2)

    drain()


def write_kernel(*refs):
    held, outs, store_sem = refs[:5], refs[5:10], refs[10]
    stores = [pltpu.make_async_copy(held[n], outs[n], store_sem.at[n]) for n in range(5)]
    for store in stores:
        store.start()
    for store in stores:
        store.wait()


def column_shards(query_rows, key_rows, value_rows, out_grad, tissue, w_out):
    N, width = query_rows.shape
    R = lax.axis_size("row")
    C = lax.axis_size("col")
    HP = H // R
    HD = width // H
    HR = R * HD
    HW = HP * HD
    T = R * N
    WQ = HW // C
    QC = 256
    vmem = pl.BlockSpec(memory_space=pltpu.VMEM)
    hbm = pl.BlockSpec(memory_space=pltpu.HBM)
    dma = pltpu.SemaphoreType.DMA
    rows = jax.ShapeDtypeStruct((N, width), BF16)
    shapes = (rows, rows, rows, rows, jax.ShapeDtypeStruct((HW, width), F32))
    operands = (tissue, query_rows, key_rows, value_rows, out_grad, w_out)
    results = pl.pallas_call(
        functools.partial(column_kernel, R, C, HP, HD, N, QC),
        out_shape=tuple(pltpu.VMEM(s.shape, s.dtype) for s in shapes),
        in_specs=[hbm] * 6,
        out_specs=(vmem,) * 5,
        scratch_shapes=[
            pltpu.SMEM(tissue.shape, jnp.int32),
            pltpu.VMEM((N, width), BF16),
            pltpu.VMEM((N, width), BF16),
            pltpu.VMEM((N, width), BF16),
            pltpu.VMEM((N, width), BF16),
            pltpu.VMEM((width, width), BF16),
            dma((4 * HP + 2,)),
            pltpu.VMEM((R, HP, 4, HD, N), BF16),
            pltpu.VMEM((HP, R, 4, HD, N), BF16),
            pltpu.VMEM((R, HP, HD, N), BF16),
            pltpu.VMEM((HP, R, HD, N), BF16),
            pltpu.VMEM((R, HP, 3, HD, N), BF16),
            pltpu.VMEM((HP, R, 3, HD, N), BF16),
            pltpu.VMEM((width, N), BF16),
            pltpu.VMEM((HP, C, R, WQ, HR), BF16),
            pltpu.VMEM((HP, C, R, WQ, HR), BF16),
            pltpu.VMEM((HP, 2, 2, WQ, HR), BF16),
            pltpu.VMEM((HP, 2, WQ, HR), BF16),
            pltpu.VMEM((HP, 2, WQ, HR), BF16),
            pltpu.VMEM((HP, WQ, HR), BF16),
            pltpu.VMEM((HP, C, WQ, HR), BF16),
            pltpu.VMEM((T, QC), F32),
            pltpu.VMEM((HP, T, T), BF16),
            pltpu.VMEM((T, T), BF16),
            pltpu.SemaphoreType.REGULAR((R,)),
            pltpu.SemaphoreType.REGULAR,
            pltpu.SemaphoreType.REGULAR,
            dma((2 * HP, R)), dma((2 * HP, R)),
            dma((HP, R)), dma((HP, R)),
            dma((HP, 3, R)), dma((HP, 3, R)),
            dma((HP, C)), dma((HP, C)),
            dma((HP,)), dma((HP,)),
            dma((HP,)), dma((HP,)),
            dma((HP, C)), dma((HP, C)),
        ],
        compiler_params=pltpu.CompilerParams(
            collective_id=0, has_side_effects=True, vmem_limit_bytes=40 * 2**20
        ),
    )(*(pltpu.with_memory_space_constraint(x, pltpu.HBM) for x in operands))
    *four, weight_t = pl.pallas_call(
        write_kernel,
        out_shape=shapes,
        in_specs=[vmem] * 5,
        out_specs=(hbm,) * 5,
        scratch_shapes=[dma((5,))],
        compiler_params=pltpu.CompilerParams(vmem_limit_bytes=2**20),
    )(*(pltpu.with_memory_space_constraint(x, pltpu.VMEM) for x in results))
    return (*four, weight_t.T)


def solution(mesh):
    in_specs = (
        P(("slides", "row", "col"), None),
        P(("slides", "row", "col"), None),
        P(("slides", "row", "col"), None),
        P(("slides", "row", "col"), None),
        P("slides"),
        P(),
    )
    out_specs = (
        P(("slides", "row", "col"), None),
        P(("slides", "row", "col"), None),
        P(("slides", "row", "col"), None),
        P(("slides", "row", "col"), None),
        P("slides", "row"),
    )
    whole_column = mesh.shape["row"] == GROUP and mesh.shape["col"] == 4
    body = column_shards if whole_column else shards
    return jax.shard_map(body, mesh=mesh, in_specs=in_specs, out_specs=out_specs, check_vma=False)
```

```python
import functools
import math

import jax
import jax.numpy as jnp
from jax import lax
from jax.experimental import pallas as pl
from jax.experimental.pallas import tpu as pltpu
from jax.sharding import PartitionSpec as P

H = 12
DILATION_STEP = 4
GROUP = 4
BLOCK = 64


NEG_FILL = -1e30


def from_behind(array, axis, by):
    devices = lax.axis_size(axis)
    pairs = [(i, i + by) for i in range(devices) if 0 <= i + by < devices]
    return lax.ppermute(array, axis, pairs)


def apply_dilation(input_array):
    head_number = input_array.shape[1]
    divide_rows = input_array.reshape(
        (input_array.shape[0] // DILATION_STEP, DILATION_STEP) + input_array.shape[1:]
    )
    return jnp.stack(
        [
            divide_rows[:, head_index % DILATION_STEP, head_index]
            for head_index in range(head_number)
        ],
        axis=1,
    )


def undilate(input_array, fill_value):
    head_number = input_array.shape[1]
    selected_rows = (
        jnp.arange(DILATION_STEP)[:, None] == (jnp.arange(head_number) % DILATION_STEP)[None, :]
    )
    selected_rows = selected_rows.reshape(
        (1, DILATION_STEP, head_number) + (1,) * (input_array.ndim - 2)
    )
    scatter_back = jnp.where(
        selected_rows, input_array[:, None], jnp.asarray(fill_value, input_array.dtype)
    )
    return scatter_back.reshape((input_array.shape[0] * DILATION_STEP,) + input_array.shape[1:])


def product(form, left, right):
    return jnp.einsum(form, left, right, preferred_element_type=jnp.float32)


def masked_scores(queries, keys_in, key_live, scale_multiplier):
    raw_scores = product("qhd,khd->hqk", queries, keys_in) * scale_multiplier
    return jnp.where(key_live.T[:, None, :] > 0, raw_scores, NEG_FILL)


def forward_rows(
    queries,
    query_live,
    band_keys,
    band_values,
    band_live,
    strip_keys,
    strip_values,
    strip_live,
    scale_multiplier,
):
    scores_band = masked_scores(queries, band_keys, band_live, scale_multiplier)
    scores_strip = masked_scores(apply_dilation(queries), strip_keys, strip_live, scale_multiplier)
    top_rows = jnp.maximum(scores_band.max(-1).T, undilate(scores_strip.max(-1).T, NEG_FILL))
    total_band = jnp.sum(jnp.exp(scores_band - top_rows.T[:, :, None]), -1).T
    total_strip = jnp.sum(jnp.exp(scores_strip - apply_dilation(top_rows).T[:, :, None]), -1).T
    logsum_total = top_rows + jnp.log(total_band + undilate(total_strip, 0.0))
    weights_band = jnp.exp(scores_band - logsum_total.T[:, :, None]).astype(jnp.bfloat16)
    weights_strip = jnp.exp(scores_strip - apply_dilation(logsum_total).T[:, :, None]).astype(
        jnp.bfloat16
    )
    combined = product("hqk,khd->qhd", weights_band, band_values)
    combined = combined + undilate(product("hqk,khd->qhd", weights_strip, strip_values), 0.0)
    return ((combined * query_live[:, None, None]).astype(jnp.bfloat16), logsum_total)


def query_branch(
    queries, grads, lse_rows, dot_rows, keys_in, values_in, key_live, scale_multiplier
):
    scores = masked_scores(queries, keys_in, key_live, scale_multiplier)
    probs = jnp.exp(scores - lse_rows.T[:, :, None])
    dprobs = product("qhd,khd->hqk", grads, values_in)
    dscores = (probs * (dprobs - dot_rows.T[:, :, None])).astype(jnp.bfloat16)
    return product("hqk,khd->qhd", dscores, keys_in)


def query_grads(
    queries,
    grads,
    lse_rows,
    dot_rows,
    band_keys,
    band_values,
    band_live,
    strip_keys,
    strip_values,
    strip_live,
    scale_multiplier,
):
    first_part = query_branch(
        queries, grads, lse_rows, dot_rows, band_keys, band_values, band_live, scale_multiplier
    )
    second_part = query_branch(
        apply_dilation(queries),
        apply_dilation(grads),
        apply_dilation(lse_rows),
        apply_dilation(dot_rows),
        strip_keys,
        strip_values,
        strip_live,
        scale_multiplier,
    )
    return ((first_part + undilate(second_part, 0.0)) * scale_multiplier).astype(jnp.bfloat16)


def key_branch(keys_in, values_in, key_live, queries, grads, lse_rows, dot_rows, scale_multiplier):
    scores = masked_scores(queries, keys_in, key_live, scale_multiplier)
    probs = jnp.exp(scores - lse_rows.T[:, :, None])
    dprobs = product("qhd,khd->hqk", grads, values_in)
    dscores = (probs * (dprobs - dot_rows.T[:, :, None])).astype(jnp.bfloat16)
    key_part = product("hqk,qhd->khd", dscores, queries)
    value_part = product("hqk,qhd->khd", probs.astype(jnp.bfloat16), grads)
    return (key_part, value_part)


def key_grads(
    keys_in,
    values_in,
    key_live,
    band_queries,
    band_grads,
    band_lse,
    band_dot,
    strip_queries,
    strip_grads,
    strip_lse,
    strip_dot,
    scale_multiplier,
):
    key_one, value_one = key_branch(
        keys_in, values_in, key_live, band_queries, band_grads, band_lse, band_dot, scale_multiplier
    )
    key_two, value_two = key_branch(
        apply_dilation(keys_in),
        apply_dilation(values_in),
        apply_dilation(key_live),
        strip_queries,
        strip_grads,
        strip_lse,
        strip_dot,
        scale_multiplier,
    )
    key_total = ((key_one + undilate(key_two, 0.0)) * scale_multiplier).astype(jnp.bfloat16)
    value_total = (value_one + undilate(value_two, 0.0)).astype(jnp.bfloat16)
    return (key_total, value_total)


def pick_members(stacked, pieces, offsets, group_pos):
    members = []
    for member in range(GROUP):
        piece = stacked
        for offset in offsets:
            piece = jnp.where(group_pos - member == offset, pieces[offset], piece)
        members.append(piece)
    return jnp.concatenate(members, 1)


def fetch_rows(stacked, row_index):
    group_pos = row_index % GROUP
    offsets = [offset for offset in range(1 - GROUP, GROUP) if offset != 0]
    pieces = {}
    for offset in offsets:
        pieces[offset] = from_behind(stacked, "row", offset)
    return pick_members(stacked, pieces, offsets, group_pos)


def fetch_stats(stacked, row_index):
    group_pos = row_index % GROUP
    offsets = [offset for offset in range(1 - GROUP, GROUP) if offset != 0]
    pieces = {}
    for offset in offsets:
        pieces[offset] = from_behind(stacked, "row", offset)
    return pick_members(stacked, pieces, offsets, group_pos)


def gather_strip(stacked):
    return lax.all_gather(stacked, "row", axis=1, tiled=True)


def shards(query_rows, key_rows, value_rows, out_grad, tissue, w_out):
    row_count, width = query_rows.shape
    head_dim = width // H
    scale_multiplier = head_dim ** (-0.5)
    row_devs = lax.axis_size("row")
    col_devs = lax.axis_size("col")
    row_index = lax.axis_index("row")
    col_index = lax.axis_index("col")
    blocks_dev = row_count // BLOCK
    device_pos = row_index * col_devs + col_index
    own_live = jnp.repeat(
        lax.dynamic_slice_in_dim(tissue, device_pos * blocks_dev, blocks_dev, 0), BLOCK
    ).astype(jnp.float32)
    column_flags = jnp.take(tissue.reshape(row_devs, col_devs, blocks_dev), col_index, axis=1)
    group_first = row_index // GROUP * GROUP
    band_blocks = lax.dynamic_slice_in_dim(column_flags, group_first, GROUP, 0).reshape(-1)
    band_flags = jnp.repeat(band_blocks, BLOCK).astype(jnp.float32)
    band_live = jnp.broadcast_to(band_flags[:, None], (GROUP * row_count, H))
    strip_flags = jnp.repeat(column_flags.reshape(-1), BLOCK).astype(jnp.float32)
    strip_live = apply_dilation(jnp.broadcast_to(strip_flags[:, None], (row_devs * row_count, H)))
    own_heads = jnp.broadcast_to(own_live[:, None], (row_count, H))
    query_per_head = query_rows.reshape(row_count, H, head_dim)
    key_per_head = key_rows.reshape(row_count, H, head_dim)
    value_per_head = value_rows.reshape(row_count, H, head_dim)
    band_pair = fetch_rows(jnp.stack([key_rows, value_rows]), row_index)
    band_keys = band_pair[0].reshape(-1, H, head_dim)
    band_values = band_pair[1].reshape(-1, H, head_dim)
    strip_pair = gather_strip(
        jnp.stack(
            [
                apply_dilation(key_per_head).reshape(-1, width),
                apply_dilation(value_per_head).reshape(-1, width),
            ]
        )
    )
    strip_keys = strip_pair[0].reshape(-1, H, head_dim)
    strip_values = strip_pair[1].reshape(-1, H, head_dim)
    attended, logsum_total = forward_rows(
        query_per_head,
        own_live,
        band_keys,
        band_values,
        band_live,
        strip_keys,
        strip_values,
        strip_live,
        scale_multiplier,
    )
    attended_rows = attended.reshape(row_count, width)
    output = jnp.dot(attended_rows, w_out, preferred_element_type=jnp.float32).astype(jnp.bfloat16)
    grad_rows = (
        jnp.dot(out_grad, w_out.T, preferred_element_type=jnp.float32) * own_live[:, None]
    ).astype(jnp.bfloat16)
    gradient_per_head = grad_rows.reshape(row_count, H, head_dim)
    score_gradient = jnp.einsum(
        "qhd,qhd->qh", gradient_per_head, attended, preferred_element_type=jnp.float32
    )
    weight_term = jnp.dot(attended_rows.T, out_grad, preferred_element_type=jnp.float32)
    weight_share = lax.psum_scatter(weight_term, "row", scatter_dimension=1, tiled=True)
    weight_grad = lax.psum(weight_share, "col")
    band_query_pair = fetch_rows(jnp.stack([query_rows, grad_rows]), row_index)
    band_stat_pair = fetch_stats(jnp.stack([logsum_total, score_gradient]), row_index)
    strip_query_pair = gather_strip(
        jnp.stack(
            [
                apply_dilation(query_per_head).reshape(-1, width),
                apply_dilation(gradient_per_head).reshape(-1, width),
            ]
        )
    )
    strip_stat_pair = lax.all_gather(
        jnp.stack([apply_dilation(logsum_total), apply_dilation(score_gradient)]),
        "row",
        axis=1,
        tiled=True,
    )
    query_grad = query_grads(
        query_per_head,
        gradient_per_head,
        logsum_total,
        score_gradient,
        band_keys,
        band_values,
        band_live,
        strip_keys,
        strip_values,
        strip_live,
        scale_multiplier,
    )
    key_grad, value_grad = key_grads(
        key_per_head,
        value_per_head,
        own_heads,
        band_query_pair[0].reshape(-1, H, head_dim),
        band_query_pair[1].reshape(-1, H, head_dim),
        band_stat_pair[0],
        band_stat_pair[1],
        strip_query_pair[0].reshape(-1, H, head_dim),
        strip_query_pair[1].reshape(-1, H, head_dim),
        strip_stat_pair[0],
        strip_stat_pair[1],
        scale_multiplier,
    )
    return (
        output,
        query_grad.reshape(row_count, width),
        key_grad.reshape(row_count, width),
        value_grad.reshape(row_count, width),
        weight_grad,
    )


MESH = pl.DeviceIdType.MESH
F32 = jnp.float32
BF16 = jnp.bfloat16


def dot_nn(a, b):
    return lax.dot_general(a, b, (((1,), (0,)), ((), ())), preferred_element_type=F32)


def dot_nt(a, b):
    return lax.dot_general(a, b, (((1,), (1,)), ((), ())), preferred_element_type=F32)


def dot_tn(a, b):
    return lax.dot_general(a, b, (((0,), (0,)), ((), ())), preferred_element_type=F32)


def column_kernel(
    R, C, HP, HD, N, QC,
    tissue_hbm, q_hbm, k_hbm, v_hbm, og_hbm, w_hbm,
    out_ref, dq_ref, dk_ref, dv_ref, wg_ref,
    tissue_ref, q_ref, k_ref, v_ref, og_ref, w_ref, load_sem,
    tx, rx, otx, orx, gtx, grx, ogt, ctx, crx, ztx, z1rx, z2tx, z2rx, frx,
    bias, probs, dsc, ready, column_in, all_in,
    a_send, a_recv, o_send, o_recv, g_send, g_recv,
    c_send, c_recv, z1_send, z1_recv, z2_send, z2_recv, f_send, f_recv,
):
    T = R * N
    HR = R * HD
    WQ = HP * HD // C
    me = lax.axis_index("row")
    col = lax.axis_index("col")
    core = col % 2
    half, parity = me // 2, me % 2
    scale = HD ** (-0.5)

    def heads(i):
        return slice(i * HR, (i + 1) * HR)

    loads = []

    def load(src, dst):
        copy = pltpu.make_async_copy(src, dst, load_sem.at[len(loads)])
        copy.start()
        loads.append(copy)
        return copy

    def load_heads(i):
        return [
            load(src.at[:, heads(i)], dst.at[:, heads(i)])
            for src, dst in ((q_hbm, q_ref), (k_hbm, k_ref), (v_hbm, v_ref))
        ]

    qkv_loads = [load_heads(0)]

    barrier = pltpu.get_barrier_semaphore()
    for d in range(1, R):
        @pl.when(me + d < R)
        def _():
            pl.semaphore_signal(barrier, inc=1, device_id={"row": me + d}, device_id_type=MESH)

    @pl.when(me == 0)
    def _():
        for d in range(1, C):
            pl.semaphore_signal(
                barrier, inc=1, device_id={"col": (col + d) % C}, device_id_type=MESH
            )

    def row_copy(src, dst, send, recv, to):
        return pltpu.make_async_remote_copy(
            src_ref=src, dst_ref=dst, send_sem=send, recv_sem=recv,
            device_id={"row": to}, device_id_type=MESH,
        )

    def col_copy(src, dst, send, recv, to):
        return pltpu.make_async_remote_copy(
            src_ref=src, dst_ref=dst, send_sem=send, recv_sem=recv,
            device_id={"col": to}, device_id_type=MESH,
        )

    pending = []

    def start(copy):
        copy.start()
        pending.append(copy)

    far = (R - 1 - me, (me + 2) % R, me + 1 - 2 * parity)
    others = (C - 1 - col, (col + 2) % C, col + 1 - 2 * core)
    twin, level = far[2], far[1]

    parcels = tuple((i, 0, 3) for i in range(HP)) + tuple((i, 3, 1) for i in range(HP))

    def parcel(n, to):
        i, a, count = parcels[n]
        return row_copy(
            tx.at[to, i, pl.ds(a, count)], rx.at[i, me, pl.ds(a, count)],
            a_send.at[n, to], a_recv.at[n, me], to,
        )

    def send_parcel(n):
        for to in far:
            start(parcel(n, to))

    def send_parcel_of(which, n):
        @pl.when(core == which)
        def _():
            for to in far:
                parcel(n, to).start()

    def sent_parcel(n):
        pending.extend(parcel(n, to) for to in far)

    def wait_parcel(n):
        i, a, count = parcels[n]
        for src in far:
            row_copy(
                tx.at[src, i, pl.ds(a, count)], rx.at[i, src, pl.ds(a, count)],
                a_send.at[n, src], a_recv.at[n, src], src,
            ).wait_recv()

    def pack_one(i, a):
        qkv_loads[i][a].wait()
        value = (q_ref, k_ref, v_ref)[a][:, heads(i)].astype(F32)
        if a == 0:
            value = value * scale
        value = value.T.astype(BF16)
        for d in range(R):
            tx[d, i, a] = value[d * HD : (d + 1) * HD]

    def pack(i):
        for a in range(3):
            pack_one(i, a)

    def live_lanes(count, first):
        lane = lax.broadcasted_iota(jnp.int32, (1, count * BLOCK), 1)
        live = jnp.zeros((1, count * BLOCK), F32)
        for j in range(count):
            live = jnp.where(lane // BLOCK == j, tissue_ref[first + j].astype(F32), live)
        return live

    def pack_grads():
        og_load.wait()
        own_live = live_lanes(per_dev, (me * C + col) * per_dev)
        for i in range(HP):
            w_loads[i].wait()
            value = (dot_nt(w_ref[heads(i), :], og_ref[...]) * own_live).astype(BF16)
            for d in range(R):
                tx[d, i, 3] = value[d * HD : (d + 1) * HD]
            rx[i, me, 3] = tx[me, i, 3]

    def turn_grads():
        ogt[...] = og_ref[...].astype(F32).T.astype(BF16)

    def wait_all_in():
        @pl.when(me > 0)
        def _():
            pl.semaphore_wait(all_in, 1)

    per_dev = N // BLOCK
    pl.semaphore_wait(barrier, jnp.where(me == 0, C - 1, me))
    for d in range(1, R):
        @pl.when(me - d >= 0)
        def _():
            pl.semaphore_signal(ready.at[me], inc=1, device_id={"row": me - d}, device_id_type=MESH)

    for a in range(3):
        pack_one(0, a)
        for d in range(R - 1, 0, -1):
            @pl.when(me - d >= 0)
            def _():
                row_copy(
                    tx.at[me - d, 0, pl.ds(a, 1)], rx.at[0, me, pl.ds(a, 1)],
                    a_send.at[0, me - d], a_recv.at[0, me], me - d,
                ).start()

    qkv_loads.append(load_heads(1))
    tissue_load = load(tissue_hbm, tissue_ref)
    og_load = load(og_hbm, og_ref)
    w_loads = [load(w_hbm.at[heads(i)], w_ref.at[heads(i)]) for i in range(HP)]
    qkv_loads.append(load_heads(2))
    for d in range(1, R):
        @pl.when(me + d < R)
        def _():
            pl.semaphore_wait(ready.at[me + d], 1)
            parcel(0, me + d).start()

    pending.extend(parcel(0, to) for to in far)
    pack(1)
    send_parcel_of(0, 1)

    @pl.when(me == 0)
    def _():
        for d in range(1, C):
            pl.semaphore_signal(
                column_in, inc=1, device_id={"col": (col + d) % C}, device_id_type=MESH
            )
        pl.semaphore_wait(column_in, C - 1)
        for d in range(1, R):
            pl.semaphore_signal(all_in, inc=1, device_id={"row": d}, device_id_type=MESH)

    pack(2)
    for i in range(HP):
        rx[i, me, 0:3] = tx[me, i, 0:3]
    tissue_load.wait()

    krow = lax.broadcasted_iota(jnp.int32, (BLOCK, QC), 0) % DILATION_STEP
    qlane = lax.broadcasted_iota(jnp.int32, (BLOCK, QC), 1) % DILATION_STEP
    twice = jnp.where((krow == me) & (qlane == me), math.log(2.0), 0.0)
    lane = lax.broadcasted_iota(jnp.int32, (1, T), 1)
    qlive = jnp.zeros((1, T), F32)
    for s in range(R):
        for b in range(per_dev):
            flag = tissue_ref[(s * C + col) * per_dev + b].astype(F32)
            j = s * per_dev + b
            bias[j * BLOCK : (j + 1) * BLOCK, :] = twice + (1.0 - flag) * NEG_FILL
            qlive = jnp.where(lane // BLOCK == j, flag, qlive)

    def gathered(i, a):
        return jnp.concatenate([rx[i, s, a] for s in range(R)], axis=1)

    attended = {}

    def forward(i):
        qt, kt, vt = gathered(i, 0), gathered(i, 1), gathered(i, 2)
        parts = []
        for c in range(T // QC):
            cols = slice(c * QC, (c + 1) * QC)
            s = dot_tn(kt, qt[:, cols]) + bias[...]
            top = jnp.max(s, axis=0, keepdims=True)
            p = jnp.exp(s - top)
            total = jnp.sum(p, axis=0, keepdims=True)
            pb = (p * (1.0 / total)).astype(BF16)
            probs[i, :, cols] = pb
            parts.append(dot_nn(vt, pb) * qlive[:, cols])
        o = jnp.concatenate(parts, axis=1).astype(BF16)
        attended[i] = o
        for d in range(R):
            otx[d, i] = o[:, d * N : (d + 1) * N]
        for to in far:
            start(row_copy(otx.at[to, i], orx.at[i, me], o_send.at[i, to], o_recv.at[i, me], to))
        orx[i, me] = otx[me, i]

    def backward(i):
        qt, kt, vt, g = (gathered(i, a) for a in range(4))
        dots = jnp.sum(g.astype(F32) * attended[i].astype(F32), axis=0, keepdims=True)
        parts = []
        for c in range(T // QC):
            cols = slice(c * QC, (c + 1) * QC)
            dp = dot_tn(vt, g[:, cols])
            ds = (probs[i, :, cols].astype(F32) * (dp - dots[:, cols])).astype(BF16)
            dsc[:, cols] = ds
            parts.append(dot_nn(kt, ds) * scale)
        results = (
            jnp.concatenate(parts, axis=1),
            dot_nt(qt, dsc[...]),
            dot_nt(g, probs[i]),
        )
        for a, value in enumerate(results):
            value = value.astype(BF16)
            for d in range(R):
                gtx[d, i, a] = value[:, d * N : (d + 1) * N]
        grx[i, me] = gtx[me, i]

    def grads_copy(i, a, count, src, dst, to):
        return row_copy(
            gtx.at[src, i, pl.ds(a, count)], grx.at[i, dst, pl.ds(a, count)],
            g_send.at[i, a, src], g_recv.at[i, a, dst], to,
        )

    splits = ((0, 3),), ((0, 1), (1, 2)), ((0, 2), (2, 1))

    def send_grads(i, part=0):
        a, count = splits[i][part]
        for to in far:
            start(grads_copy(i, a, count, to, me, to))

    def send_grads_of(which, i, part=0):
        a, count = splits[i][part]

        order = far if i < HP - 1 else [jnp.where(d < me, d, d + 1) for d in range(R - 1)]

        @pl.when(core == which)
        def _():
            for to in order:
                grads_copy(i, a, count, to, me, to).start()

    def sent_grads(i):
        for a, count in splits[i]:
            pending.extend(grads_copy(i, a, count, to, me, to) for to in far)

    def wait_o(i):
        for src in far:
            row_copy(
                otx.at[src, i], orx.at[i, src], o_send.at[i, src], o_recv.at[i, src], src
            ).wait_recv()

    def weight_core(i):
        wait_o(i)
        term = dot_nt(ogt[...], orx[i].reshape(HR, N)).astype(BF16)
        for r in range(R):
            for c in range(C):
                first = (r * C + c) * WQ
                ctx[i, c, r] = term[first : first + WQ]
        for to in others:
            start(col_copy(ctx.at[i, to], crx.at[i, col], c_send.at[i, to], c_recv.at[i, col], to))

    def wait_c(i):
        for src in others:
            col_copy(
                ctx.at[i, src], crx.at[i, src], c_send.at[i, src], c_recv.at[i, src], src
            ).wait_recv()

    def weight_twin(i):
        wait_c(i)
        share = ctx[i, col].astype(F32)
        for src in others:
            share = share + crx[i, src].astype(F32)
        share = share.astype(BF16)
        for r in range(R):
            ztx[i, r % 2, r // 2] = share[r]
        start(row_copy(ztx.at[i, 1 - parity], z1rx.at[i], z1_send.at[i], z1_recv.at[i], twin))

    def wait_z1(i):
        row_copy(ztx.at[i, 1 - parity], z1rx.at[i], z1_send.at[i], z1_recv.at[i], twin).wait_recv()

    def weight_level(i):
        wait_z1(i)
        z2tx[i] = (ztx[i, parity].astype(F32) + z1rx[i].astype(F32)).astype(BF16)
        start(row_copy(z2tx.at[i, 1 - half], z2rx.at[i], z2_send.at[i], z2_recv.at[i], level))

    def wait_z2(i):
        row_copy(z2tx.at[i, 1 - half], z2rx.at[i], z2_send.at[i], z2_recv.at[i], level).wait_recv()

    def weight_spread(i):
        wait_z2(i)
        frx[i, col] = (z2tx[i, half].astype(F32) + z2rx[i].astype(F32)).astype(BF16)
        for to in others:
            start(col_copy(frx.at[i, col], frx.at[i, col], f_send.at[i, to], f_recv.at[i, col], to))

    def wait_f(i):
        for src in others:
            col_copy(
                frx.at[i, src], frx.at[i, src], f_send.at[i, src], f_recv.at[i, src], src
            ).wait_recv()

    def weight_write(i):
        wait_f(i)
        wg_ref[:, heads(i)] = frx[i].reshape(C * WQ, HR).astype(F32)

    def wait_part(i, a, count):
        for src in far:
            grads_copy(i, a, count, src, src, src).wait_recv()

    def wait_g(i):
        for a, count in splits[i]:
            wait_part(i, a, count)

    def grads_write(i):
        refs = (dq_ref, dk_ref, dv_ref)
        for first, count in splits[i]:
            wait_part(i, first, count)
            for a in range(first, first + count):
                value = grx[i, :, a].reshape(HR, N)
                refs[a][:, heads(i)] = value.astype(F32).T.astype(BF16)

    def drain():
        for copy in pending:
            copy.wait_send()
        pending.clear()

    pack_grads()
    turn_grads()
    wait_parcel(0)
    forward(0)
    send_parcel_of(1, 1)
    wait_all_in()
    sent_parcel(1)
    send_parcel_of(0, 2)
    wait_parcel(1)
    forward(1)
    send_parcel_of(1, 2)
    send_parcel(3)
    weight_core(0)
    wait_parcel(2)
    forward(2)
    send_parcel(4)
    weight_core(1)
    send_parcel(5)
    wait_parcel(3)
    backward(0)
    send_grads_of(0, 0, 0)
    send_grads_of(1, 0, 0)
    weight_core(2)
    weight_twin(0)
    wait_parcel(4)
    backward(1)
    weight_level(0)
    send_grads_of(0, 1, 0)
    send_grads_of(1, 1, 0)
    send_grads_of(0, 1, 1)
    weight_twin(1)
    wait_parcel(5)
    backward(2)
    send_grads_of(1, 1, 1)
    weight_twin(2)
    weight_level(1)
    weight_level(2)
    send_grads_of(0, 2, 0)
    send_grads_of(1, 2, 0)
    send_grads_of(0, 2, 1)
    send_grads_of(1, 2, 1)
    sent_parcel(2)
    sent_grads(0)
    sent_grads(1)
    weight_spread(0)
    out_ref[...] = dot_tn(orx[...].reshape(HP * HR, N), w_ref[...]).astype(BF16)
    weight_spread(1)
    weight_spread(2)
    grads_write(0)
    grads_write(1)
    weight_write(0)
    weight_write(1)
    weight_write(2)
    drain()
    sent_grads(2)
    grads_write(2)

    drain()


def write_kernel(*refs):
    held, outs, store_sem = refs[:5], refs[5:10], refs[10]
    stores = [pltpu.make_async_copy(held[n], outs[n], store_sem.at[n]) for n in range(5)]
    for store in stores:
        store.start()
    for store in stores:
        store.wait()


def column_shards(query_rows, key_rows, value_rows, out_grad, tissue, w_out):
    N, width = query_rows.shape
    R = lax.axis_size("row")
    C = lax.axis_size("col")
    HP = H // R
    HD = width // H
    HR = R * HD
    HW = HP * HD
    T = R * N
    WQ = HW // C
    QC = 256
    vmem = pl.BlockSpec(memory_space=pltpu.VMEM)
    hbm = pl.BlockSpec(memory_space=pltpu.HBM)
    dma = pltpu.SemaphoreType.DMA
    rows = jax.ShapeDtypeStruct((N, width), BF16)
    shapes = (rows, rows, rows, rows, jax.ShapeDtypeStruct((HW, width), F32))
    operands = (tissue, query_rows, key_rows, value_rows, out_grad, w_out)
    results = pl.pallas_call(
        functools.partial(column_kernel, R, C, HP, HD, N, QC),
        out_shape=tuple(pltpu.VMEM(s.shape, s.dtype) for s in shapes),
        in_specs=[hbm] * 6,
        out_specs=(vmem,) * 5,
        scratch_shapes=[
            pltpu.SMEM(tissue.shape, jnp.int32),
            pltpu.VMEM((N, width), BF16),
            pltpu.VMEM((N, width), BF16),
            pltpu.VMEM((N, width), BF16),
            pltpu.VMEM((N, width), BF16),
            pltpu.VMEM((width, width), BF16),
            dma((4 * HP + 2,)),
            pltpu.VMEM((R, HP, 4, HD, N), BF16),
            pltpu.VMEM((HP, R, 4, HD, N), BF16),
            pltpu.VMEM((R, HP, HD, N), BF16),
            pltpu.VMEM((HP, R, HD, N), BF16),
            pltpu.VMEM((R, HP, 3, HD, N), BF16),
            pltpu.VMEM((HP, R, 3, HD, N), BF16),
            pltpu.VMEM((width, N), BF16),
            pltpu.VMEM((HP, C, R, WQ, HR), BF16),
            pltpu.VMEM((HP, C, R, WQ, HR), BF16),
            pltpu.VMEM((HP, 2, 2, WQ, HR), BF16),
            pltpu.VMEM((HP, 2, WQ, HR), BF16),
            pltpu.VMEM((HP, 2, WQ, HR), BF16),
            pltpu.VMEM((HP, WQ, HR), BF16),
            pltpu.VMEM((HP, C, WQ, HR), BF16),
            pltpu.VMEM((T, QC), F32),
            pltpu.VMEM((HP, T, T), BF16),
            pltpu.VMEM((T, T), BF16),
            pltpu.SemaphoreType.REGULAR((R,)),
            pltpu.SemaphoreType.REGULAR,
            pltpu.SemaphoreType.REGULAR,
            dma((2 * HP, R)), dma((2 * HP, R)),
            dma((HP, R)), dma((HP, R)),
            dma((HP, 3, R)), dma((HP, 3, R)),
            dma((HP, C)), dma((HP, C)),
            dma((HP,)), dma((HP,)),
            dma((HP,)), dma((HP,)),
            dma((HP, C)), dma((HP, C)),
        ],
        compiler_params=pltpu.CompilerParams(
            collective_id=0, has_side_effects=True, vmem_limit_bytes=40 * 2**20
        ),
    )(*(pltpu.with_memory_space_constraint(x, pltpu.HBM) for x in operands))
    *four, weight_t = pl.pallas_call(
        write_kernel,
        out_shape=shapes,
        in_specs=[vmem] * 5,
        out_specs=(hbm,) * 5,
        scratch_shapes=[dma((5,))],
        compiler_params=pltpu.CompilerParams(vmem_limit_bytes=2**20),
    )(*(pltpu.with_memory_space_constraint(x, pltpu.VMEM) for x in results))
    return (*four, weight_t.T)


def solution(mesh):
    in_specs = (
        P(("slides", "row", "col"), None),
        P(("slides", "row", "col"), None),
        P(("slides", "row", "col"), None),
        P(("slides", "row", "col"), None),
        P("slides"),
        P(),
    )
    out_specs = (
        P(("slides", "row", "col"), None),
        P(("slides", "row", "col"), None),
        P(("slides", "row", "col"), None),
        P(("slides", "row", "col"), None),
        P("slides", "row"),
    )
    whole_column = mesh.shape["row"] == GROUP and mesh.shape["col"] == 4
    body = column_shards if whole_column else shards
    return jax.shard_map(body, mesh=mesh, in_specs=in_specs, out_specs=out_specs, check_vma=False)
```
